32 devices in a mesh: tm: 16 (over z, y, x), space: 2 (over core).
Axes of the slice: x: 2, y: 2, z: 4, core: 2. Of those that a mesh axis runs over, the one named last changes fastest.
Arguments:
- snapshots: bfloat16 [8192, 16384], P('tm', 'space'), may hold values from -40 to 40
- exponents: float32 [2, 32], replicated, may hold values from -150 to 150, as said below
Outputs:
- new_exponents: float32 [2, 32], replicated
- amplitudes: float32 [2, 32, 16384], P(None, None, 'space')
- residual: bfloat16 [8192, 16384], P('tm', 'space')
The draws below stay inside these ranges and needn't reach their ends.
Inputs may be any that keep to these rules, and one draw needn't show every extreme that they name: `exponents`: row 0 lies in -2.3 to 0.8, row 1 in -150 to 150.
All inputs are finite; a program needn't handle non-finite values.
Results may differ from the reference program's by a relative error of at most 0.0012.
The reference program's roundings to bfloat16 on the way count: a program that leaves them out, or rounds other values in their place, can miss the bound.
Values sent between devices are 32-bit elements; how exact they have to be, the bound alone decides.
A program may use at most 64 MiB of HBM per device.

```python
import math
import jax
import jax.numpy as jnp
from jax import lax

MODES = 32
TIMES = 8192
SPACE = 16384


def true_modes(key):
    base = jax.random.fold_in(key, 7)
    first_key, second_key = jax.random.split(base)
    decay_rates = jax.random.uniform(first_key, (MODES,), jnp.float32, -2.0, 0.5)
    spacing = 2.0 * math.pi * 1.5
    frequencies = spacing * (jnp.arange(MODES, dtype=jnp.float32) - (MODES - 1) / 2.0)
    frequencies = frequencies + jax.random.uniform(second_key, (MODES,), jnp.float32, -2.0, 2.0)
    return (decay_rates, frequencies)


def draw_exponents(key, part):
    decay_rates, frequencies = true_modes(key)
    first_key, second_key = jax.random.split(jax.random.fold_in(key, 19))
    shifted_rates = decay_rates + jax.random.uniform(first_key, (MODES,), jnp.float32, -0.3, 0.3)
    shifted_freqs = frequencies + jax.random.uniform(second_key, (MODES,), jnp.float32, -0.5, 0.5)
    return jnp.stack([shifted_rates, shifted_freqs]).astype(jnp.float32)


def draw_snapshots(key, part):
    decay_rates, frequencies = true_modes(key)
    time_grid = jnp.arange(TIMES, dtype=jnp.int32).astype(jnp.float32) / TIMES
    first_key, second_key = jax.random.split(jax.random.fold_in(key, 23))
    column_pos = jnp.arange(SPACE, dtype=jnp.int32).astype(jnp.float32) / SPACE
    column_scale = 0.15 * (1.0 + 2.0 * column_pos)
    amp_real = jax.random.normal(first_key, (MODES, SPACE), jnp.float32) * column_scale[None, :]
    amp_imag = jax.random.normal(second_key, (MODES, SPACE), jnp.float32) * column_scale[None, :]
    region = jnp.arange(SPACE, dtype=jnp.int32) * 4 // SPACE
    model_part = jnp.zeros((TIMES, SPACE), jnp.float32)
    for quarter in range(4):
        offset = quarter - 1.5
        magnitude = jnp.exp(time_grid[:, None] * (decay_rates + 0.2 * offset)[None, :])
        phase_angle = time_grid[:, None] * (frequencies + 0.8 * offset)[None, :]
        inside = (region == quarter).astype(jnp.float32)[None, :]
        model_part = model_part + jnp.dot(magnitude * jnp.cos(phase_angle), amp_real * inside, precision=lax.Precision.HIGHEST)
        model_part = model_part - jnp.dot(magnitude * jnp.sin(phase_angle), amp_imag * inside, precision=lax.Precision.HIGHEST)
    noise_field = 0.5 * jax.random.normal(jax.random.fold_in(key, 29), (TIMES, SPACE), jnp.float32)
    return jnp.clip(model_part + noise_field, -40.0, 40.0).astype(jnp.bfloat16)


def setup_inputs(seed: int = 0) -> dict:
    key_of = jax.random.split(jax.random.key(seed), 3)
    return {
        "snapshots": draw_snapshots(jax.random.fold_in(key_of[2], 71), 0),
        "exponents": draw_exponents(jax.random.fold_in(key_of[2], 71), 0),
    }


damping = 0.01

def factor_solve(factor, right):
    lower_part = lax.linalg.triangular_solve(factor, right, left_side=True, lower=True)
    return lax.linalg.triangular_solve(factor, lower_part, left_side=True, lower=True, transpose_a=True)

def make_basis(exponents, time_grid):
    magnitude = jnp.exp(time_grid[:, None] * exponents[0][None, :])
    phase_angle = time_grid[:, None] * exponents[1][None, :]
    plain = jnp.concatenate([magnitude * jnp.cos(phase_angle), magnitude * jnp.sin(phase_angle)], 1)
    return jnp.concatenate([plain, time_grid[:, None] * plain], 1)

def inner_product(left, right):
    return lax.dot_general(left.astype(jnp.float32), right.astype(jnp.float32), (((0,), (0,)), ((), ())), precision=lax.Precision.HIGHEST, preferred_element_type=jnp.float32)

def hermitian(blocks, modes):
    return (blocks[:modes, :modes] + blocks[modes:, modes:], blocks[:modes, modes:] - blocks[modes:, :modes])

def embedded(real_part, imag_part):
    return jnp.concatenate([jnp.concatenate([real_part, -imag_part], 1), jnp.concatenate([imag_part, real_part], 1)], 0)

def sign_flip(modes):
    return jnp.concatenate([jnp.ones((modes,), jnp.float32), -jnp.ones((modes,), jnp.float32)])

def basis_solve(gram_matrix, modes):
    double = 2 * modes
    g_real, g_imag = hermitian(gram_matrix[:double, :double], modes)
    factor = jnp.linalg.cholesky(embedded(g_real, g_imag))
    return factor_solve(factor, jnp.eye(double, dtype=jnp.float32))

def amplitude_rows(inverse_g, projections, modes):
    left_solve = inverse_g * sign_flip(modes)[None, :]
    return lax.dot_general(left_solve.astype(jnp.float32), projections[:, :2 * modes].astype(jnp.float32), (((1,), (1,)), ((), ())), precision=lax.Precision.HIGHEST, preferred_element_type=jnp.float32)

def fit_terms(amp_rows, projections, modes):
    double = 2 * modes
    self_terms = lax.dot_general(amp_rows.astype(jnp.float32), amp_rows.astype(jnp.float32), (((1,), (1,)), ((), ())), precision=lax.Precision.HIGHEST, preferred_element_type=jnp.float32)
    cross = jnp.dot(amp_rows.astype(jnp.float32), projections[:, double:].astype(jnp.float32), precision=lax.Precision.HIGHEST, preferred_element_type=jnp.float32) * sign_flip(modes)[None, :]
    v_real = jnp.diagonal(cross[:modes, :modes]) + jnp.diagonal(cross[modes:, modes:])
    v_imag = jnp.diagonal(cross[:modes, modes:]) - jnp.diagonal(cross[modes:, :modes])
    return (self_terms, jnp.stack([v_real, v_imag]))

def lm_update(exponents, gram_matrix, inverse_g, self_terms, cross_sums, modes):
    double = 2 * modes
    c_real, c_imag = hermitian(gram_matrix[:double, double:], modes)
    e_real, e_imag = hermitian(gram_matrix[double:, double:], modes)
    coupling = embedded(c_real, c_imag)
    through = jnp.dot(coupling.T, inverse_g, precision=lax.Precision.HIGHEST)
    reduced = embedded(e_real, e_imag) - jnp.dot(through, coupling, precision=lax.Precision.HIGHEST)
    m_real = reduced[:modes, :modes]
    m_imag = reduced[modes:, :modes]
    s_real, s_imag = hermitian(self_terms, modes)
    w_real = jnp.sum(c_real.T * s_real + c_imag.T * s_imag, 1)
    w_imag = jnp.sum(c_real.T * s_imag - c_imag.T * s_real, 1)
    grad_real = w_real - cross_sums[0]
    grad_imag = w_imag - cross_sums[1]
    h_real = s_real * m_real - s_imag * m_imag + damping * jnp.eye(modes, dtype=jnp.float32)
    h_imag = s_real * m_imag + s_imag * m_real
    factor = jnp.linalg.cholesky(embedded(h_real, h_imag))
    step_vector = factor_solve(factor, jnp.concatenate([grad_real, grad_imag])[:, None])[:, 0]
    return exponents - jnp.stack([step_vector[:modes], step_vector[modes:]])

def reference(snapshots, exponents):
    modes = MODES
    time_grid = jnp.arange(TIMES, dtype=jnp.int32).astype(jnp.float32) / TIMES
    basis = make_basis(exponents, time_grid)
    gram_matrix = inner_product(basis, basis)
    basis_b = basis.astype(jnp.bfloat16)
    projections = lax.dot_general(snapshots.astype(jnp.float32), basis_b.astype(jnp.float32), (((0,), (0,)), ((), ())), preferred_element_type=jnp.float32)
    inverse_g = basis_solve(gram_matrix, modes)
    amp_rows = amplitude_rows(inverse_g, projections, modes)
    self_terms, cross_sums = fit_terms(amp_rows, projections, modes)
    new_exponents = lm_update(exponents, gram_matrix, inverse_g, self_terms, cross_sums, modes)
    signed = (amp_rows * sign_flip(modes)[:, None]).astype(jnp.bfloat16)
    fitted = jnp.dot(basis_b[:, :2 * modes].astype(jnp.float32), signed.astype(jnp.float32), preferred_element_type=jnp.float32)
    residual = (snapshots.astype(jnp.float32) - fitted).astype(jnp.bfloat16)
    return (new_exponents, amp_rows.reshape(2, modes, SPACE), residual)
```

```python
import functools
import heapq

import jax
import jax.numpy as jnp
from jax import lax
from jax.experimental import pallas as pl
from jax.experimental.pallas import tpu as pltpu
from jax.sharding import PartitionSpec as P

damping = 0.01
MESH = pl.DeviceIdType.MESH
LANES = 128
TILE = 512
FIT_TILE = 256
INVERT_STEPS = 4
ORDERS = (
    (1, 2, 0), (2, 0, 1), (0, 1, 2), (1, 2, 0), (0, 2, 1), (1, 2, 0), (1, 0, 2), (0, 1, 2),
)
OVER_LANES = ((1,), (1,))

LINK_BYTES_PER_US = 100e3
HOP_US = 2.3
FAR_US = 0.5
STEP_US = 0.15
PROJECT_US = 0.25
AMPLITUDE_US = 0.5
GRAM_US = 1.2
INVERT_US = 0.4
MODEL_US = 1.0
CROSS_US = 0.15
FIT_US = 0.35
START_US = 1.5


def exact_dot(left, right, dims=((1,), (0,))):
    return lax.dot_general(
        left,
        right,
        (dims, ((), ())),
        precision=lax.Precision.HIGHEST,
        preferred_element_type=jnp.float32,
    )


def complex_dot(ar, ai, br, bi):
    return exact_dot(ar, br) - exact_dot(ai, bi), exact_dot(ar, bi) + exact_dot(ai, br)


def complex_product(ar, ai, br, bi):
    return ar * br - ai * bi, ar * bi + ai * br


def invert_steps(real, imag, first, count):
    rows = lax.broadcasted_iota(jnp.int32, real.shape, 0)
    cols = lax.broadcasted_iota(jnp.int32, real.shape, 1)
    for k in range(first, first + count):
        on_row, on_col = rows == k, cols == k
        scale = 1.0 / real[k : k + 1, k : k + 1]
        row_r = jnp.where(on_col[:1], 1.0, real[k : k + 1, :]) * scale
        row_i = jnp.where(on_col[:1], 0.0, imag[k : k + 1, :]) * scale
        col_r, col_i = real[:, k : k + 1], imag[:, k : k + 1]
        real = jnp.where(
            on_row, row_r, jnp.where(on_col, 0.0, real) - (col_r * row_r - col_i * row_i)
        )
        imag = jnp.where(
            on_row, row_i, jnp.where(on_col, 0.0, imag) - (col_r * row_i + col_i * row_r)
        )
    return real, imag


def column_of(row):
    n = row.shape[1]
    here = lax.broadcasted_iota(jnp.int32, (n, n), 0) == lax.broadcasted_iota(
        jnp.int32, (n, n), 1
    )
    return jnp.sum(jnp.where(here, row, 0.0), 1, keepdims=True)


def waves(rate, frequency, time):
    magnitude = jnp.exp(time * rate)
    angle = time * frequency
    return magnitude * jnp.cos(angle), magnitude * jnp.sin(angle)


def moments(real, imag, time):
    modes = real.shape[0]
    both = jnp.concatenate(
        [jnp.concatenate([real, imag], 1), jnp.concatenate([-imag, real], 1)], 0
    )
    first, twice = both[:modes], jnp.concatenate([time, time], 1)
    powers = [first, twice * first, twice * (twice * first)]
    powers += [jnp.zeros_like(first)] * (LANES // modes - len(powers))
    sums = exact_dot(both, jnp.concatenate(powers, 0), OVER_LANES)
    blocks = []
    for n in range(3):
        moved = sums if n == 0 else pltpu.roll(sums, LANES - n * modes, 1)
        blocks.append((moved[:modes, :modes], moved[modes:, :modes]))
    return blocks


def timeline(orders, bits, width, rows, invert_jobs):
    parts, last = len(orders), 2 * bits - 2
    free = {}
    events, script, count = [], [], [0]
    done = set()
    now = START_US

    def post(at, what):
        heapq.heappush(events, (at, count[0], what))
        count[0] += 1

    def send(p, stage):
        s = min(stage, last - stage)
        bit = orders[p][s]
        size = (width >> min(s + 1, bits - 1)) * rows * 4 / LINK_BYTES_PER_US
        delay = HOP_US
        if bit < 2:
            keys = {"xy": size}
        elif bit == 2:
            keys = {"near": 2 * size}
        else:
            keys, delay = {"near": 2 * size, "far": 4 * size}, HOP_US + FAR_US
        start = max([now] + [free.get(k, 0.0) for k in keys])
        for k, v in keys.items():
            free[k] = start + v
        post(start + max(keys.values()) + delay, ("arrive", p, stage))

    for p in range(parts):
        now += PROJECT_US
        send(p, 0)
    jobs = [("rest", p) for p in range(parts)] + [("gram",)]
    jobs += [("invert", i) for i in range(invert_jobs)] + [("model",)]
    cost = {
        "rest": PROJECT_US, "gram": GRAM_US, "invert": INVERT_US, "model": MODEL_US,
        "hessian": INVERT_US, "cross": CROSS_US, "fit": FIT_US,
    }
    rank = {
        "rest": 0, "gram": 1, "invert": 2, "cross": 3, "hessian": 4, "model": 5, "fit": 6,
    }

    def run(job):
        nonlocal now
        jobs.remove(job)
        done.add(job)
        script.append(job)
        now += cost[job[0]]

    amplitudes = crossed = 0
    while events or jobs:
        if events and (events[0][0] <= now or not jobs):
            at, _, what = heapq.heappop(events)
            now = max(now, at)
            if what[0] == "arrive":
                _, p, stage = what
                if stage == 0 and ("rest", p) not in done:
                    run(("rest", p))
                if stage == bits - 1:
                    for job in [j for j in jobs if j[0] in ("gram", "invert")]:
                        run(job)
                    now += AMPLITUDE_US
                    amplitudes += 1
                script.append(what)
                now += STEP_US
                if stage < last:
                    send(p, stage + 1)
                if stage >= last - 1:
                    k = stage - (last - 1)
                    jobs += [("cross", p, k), ("fit", p, k)]
                if amplitudes == parts and ("sum",) not in done:
                    done.add(("sum",))
                    script.append(("sum",))
                    now += AMPLITUDE_US
                    post(now + HOP_US + 1.0, ("sum_near",))
            elif what[0] == "sum_near":
                script.append(what)
                now += STEP_US
                post(now + HOP_US, ("sum_far",))
            else:
                script.append(what)
                if ("model",) in jobs:
                    jobs.remove(("model",))
                    script.insert(len(script) - 1, ("model",))
                jobs += [("hessian", i) for i in range(invert_jobs)]
            continue
        job = min(jobs, key=lambda j: rank[j[0]])
        if events and rank[job[0]] > 2 and events[0][0] < now + 0.05:
            now = events[0][0]
            continue
        run(job)
        if job[0] == "cross":
            crossed += 1
            if crossed == 2 * parts:
                script.append(("cross_sum",))
    return script


def step_kernel(
    modes, tm_bits, sp_bits, parts,
    x_ref, exps_ref,
    full, res_ref, new_ref,
    xbuf, yz_ref, basis, fit_basis, halves, tail, ssum, snear, sfar, vsum, vnear, vfar,
    rs_send, rs_recv, ag_send, ag_recv,
    sn_send, sn_recv, sf_send, sf_recv, n_send, n_recv, f_send, f_recv, x_sem,
):
    double = 2 * modes
    local_rows, columns = xbuf.shape
    width = columns // parts
    half = width // 2
    last = tm_bits - 1
    me, sp = lax.axis_index("tm"), lax.axis_index("space")
    swap = sp % 2

    def stride_of(bit):
        if tm_bits > 2 and bit == 0:
            return 1 + swap
        if tm_bits > 2 and bit == 1:
            return 2 - swap
        return 2**bit

    def flip(index, stride):
        side = (index // stride) % 2
        return side, index + (1 - 2 * side) * stride

    spaces, low = 2**sp_bits, 2 ** (tm_bits // 2)
    n_near, n_far = low * spaces, 2**tm_bits // low
    n_mid = n_far // 2
    near_slot, far_slot = (me % low) * spaces + sp, me // low
    mid_slot = far_slot % n_mid
    near, mid, far = [], [], []
    for d in range(1, n_near):
        other = (near_slot + d) % n_near
        near.append((far_slot * low + other // spaces, other % spaces))
    for d in range(1, n_mid):
        other = (far_slot // n_mid) * n_mid + (mid_slot + d) % n_mid
        mid.append((other * low + me % low, sp))
    for d in range(1, n_far):
        far.append(((far_slot + d) % n_far * low + me % low, sp))

    def lanes(start, size):
        return pl.ds(pl.multiple_of(start, LANES), size)

    orders = []
    for p in range(parts):
        order = [b for b in ORDERS[p % len(ORDERS)] if b < last]
        orders.append(order + [b for b in range(tm_bits) if b not in order])
    plan = [[flip(me, stride_of(b)) for b in order] for order in orders]

    def part_half(p, k):
        side = plan[p][0][0]
        return p * width + ((1 - side) * half if k == 0 else side * half)

    loads = {}
    for k in range(2):
        for p in range(parts):
            at = lanes(part_half(p, k), half)
            loads[p, k] = pltpu.make_async_copy(x_ref.at[:, at], xbuf.at[:, at], x_sem.at[p, k])
            loads[p, k].start()

    barrier = pltpu.get_barrier_semaphore()
    for friend in near + far:
        pl.semaphore_signal(barrier, inc=1, device_id=friend, device_id_type=MESH)

    rate, frequency = column_of(exps_ref[pl.ds(0, 1), :]), column_of(exps_ref[pl.ds(1, 1), :])
    total_rows = local_rows * 2**tm_bits
    steps = lax.broadcasted_iota(jnp.int32, (1, local_rows), 1)
    time = (me * local_rows + steps).astype(jnp.float32) / total_rows
    real, imag = waves(rate, frequency, time)
    plain = jnp.concatenate([real, -imag], 0)
    basis[...] = jnp.concatenate([plain, time * plain], 0).astype(jnp.bfloat16)

    def project(p, k):
        loads[p, k].wait()
        at = part_half(p, k)
        tile = min(TILE, half)

        def step(i, carry):
            here = lanes(at + i * tile, tile)
            yz_ref[:, here] = jnp.dot(
                basis[...], xbuf[:, here], preferred_element_type=jnp.float32
            )
            return carry

        lax.fori_loop(0, half // tile, step, 0)

    sends = []

    def remote(src, dst, send, recv, friend):
        copy = pltpu.make_async_remote_copy(
            src_ref=src, dst_ref=dst, send_sem=send, recv_sem=recv,
            device_id=friend, device_id_type=MESH,
        )
        copy.start()
        sends.append(copy)
        return copy

    flying = {}
    above = pl.ds(0, double)

    def scatter_start(p, s):
        side, partner = plan[p][s]
        size = width >> (s + 1)
        away = (1 - side) * size
        if s == last:
            src, dst = halves[s - 1].at[p], tail.at[p]
        elif s == 0:
            src, dst = yz_ref.at[above, lanes(p * width + away, size)], halves[s].at[p]
        else:
            src, dst = halves[s - 1].at[p, :, lanes(away, size)], halves[s].at[p]
        flying[p] = remote(src, dst, rs_send.at[p, s], rs_recv.at[p, s], (partner, sp))

    def scatter_add(p, s):
        side, _ = plan[p][s]
        size = width >> (s + 1)
        if s == 0:
            mine = yz_ref[above, lanes(p * width + side * size, size)]
        else:
            mine = halves[s - 1][p, :, lanes(side * size, size)]
        halves[s][p] = halves[s][p] + mine

    offsets = []
    for p in range(parts):
        start = p * width
        for s in range(last):
            start = start + plan[p][s][0] * (width >> (s + 1))
        offsets.append(start)

    def gather_start(p, s):
        where = full.at[:, lanes(offsets[p], width >> (s + 1))]
        flying[p] = remote(
            where, where, ag_send.at[p, s], ag_recv.at[p, s], (plan[p][s][1], sp)
        )

    def gather_sum_start(source, landed, slot, peers, send, recv):
        copies = [
            remote(source, landed.at[slot], send.at[d], recv.at[d], peer)
            for d, peer in enumerate(peers)
        ]
        landed[slot] = source[...]
        return copies

    def gather_sum_end(copies, landed):
        for copy in copies:
            copy.wait_recv()
        total = landed[0]
        for k in range(1, len(copies) + 1):
            total = total + landed[k]
        return total

    for p in range(parts):
        project(p, 0)
        if p == 0:
            pl.semaphore_wait(barrier, len(near + far))
        scatter_start(p, 0)

    state = {
        "self": jnp.zeros((double, double), jnp.float32),
        "cross": (jnp.zeros((modes, LANES), jnp.float32),) * 2,
    }
    square = (modes, modes)

    def gram():
        fit_basis[...] = jnp.transpose(plain).astype(jnp.bfloat16)
        base_time = steps.astype(jnp.float32) / total_rows
        base = moments(*waves(rate, frequency, base_time), base_time)
        groups = 2**tm_bits
        wide = max(LANES, groups)
        block = lax.broadcasted_iota(jnp.int32, (1, wide), 1)
        shift_time = (block * local_rows).astype(jnp.float32) / total_rows
        used = block < groups
        shift_time = jnp.where(used, shift_time, 0.0)
        turn_r, turn_i = waves(rate, frequency, shift_time)
        turn = moments(
            jnp.where(used, turn_r, 0.0), jnp.where(used, turn_i, 0.0), shift_time
        )

        def times(m, n):
            return complex_product(*turn[m], *base[n])

        g = times(0, 0)
        c = [a + b for a, b in zip(times(1, 0), times(0, 1))]
        e = [
            a + 2.0 * b + d for a, b, d in zip(times(2, 0), times(1, 1), times(0, 2))
        ]
        state.update(c=c, e=e, inverse=g)

    def finish_inverse():
        inv_r, inv_i = state["inverse"]
        state["solve"] = jnp.concatenate(
            [jnp.concatenate([inv_r, -inv_i], 1), jnp.concatenate([inv_i, inv_r], 1)], 0
        )

    def model():
        c_r, c_i = state["c"]
        t_r, t_i = complex_dot(*state["inverse"], c_r, c_i)
        u_r, u_i = complex_dot(c_r, c_i, t_r, t_i)
        state["m"] = (state["e"][0] - u_r, state["e"][1] - u_i)

    def arrive(p, stage):
        if stage < last:
            flying[p].wait_recv()
            scatter_add(p, stage)
            scatter_start(p, stage + 1)
        elif stage == last:
            flying[p].wait_recv()
            amps = exact_dot(state["solve"], halves[last - 1][p] + tail[p])
            full[:, lanes(offsets[p], width >> last)] = amps
            gather_start(p, last - 1)
            state["self"] = state["self"] + exact_dot(amps, amps, OVER_LANES)
        else:
            s = 2 * last - stage
            flying[p].wait_recv()
            offsets[p] = offsets[p] - plan[p][s][0] * (width >> (s + 1))
            if s > 0:
                gather_start(p, s - 1)

    def sum_start():
        both = state["self"]
        moved = pltpu.roll(jnp.concatenate([both, both], 1), LANES - modes, 1)
        s_r = both[:modes, :modes] + moved[modes:, :modes]
        s_i = moved[:modes, :modes] - both[modes:, :modes]
        pair = jnp.concatenate([s_r, s_i], 1)
        ssum[0] = jnp.concatenate([pair[: modes // 2], pair[modes // 2 :]], 1)
        state["copies"] = gather_sum_start(ssum.at[0], snear, near_slot, near, sn_send, sn_recv)

    def sum_near():
        ssum[1] = gather_sum_end(state["copies"], snear)
        state["copies"] = gather_sum_start(ssum.at[1], sfar, mid_slot, mid, sf_send, sf_recv)

    def sum_far():
        packed = gather_sum_end(state["copies"], sfar)

        def piece(n):
            moved = packed if n == 0 else pltpu.roll(packed, LANES - n * modes, 1)
            return moved[:, :modes]

        s_r = jnp.concatenate([piece(0), piece(2)], 0)
        s_i = jnp.concatenate([piece(1), piece(3)], 0)
        diagonal = lax.broadcasted_iota(jnp.int32, square, 0) == lax.broadcasted_iota(
            jnp.int32, square, 1
        )
        h_r, h_i = complex_product(s_r, s_i, *state["m"])
        c_r, c_i = state["c"]
        state["hessian"] = (h_r + jnp.where(diagonal, damping, 0.0), h_i)
        state["w"] = (
            jnp.sum(c_r * s_r - c_i * s_i, 1, keepdims=True),
            jnp.sum(c_r * s_i + c_i * s_r, 1, keepdims=True),
        )

    def fit_start(p, k):
        return part_half(p, 1 - k)

    def cross(p, k):
        start = fit_start(p, k)
        run = min(4, half // LANES)

        def step(i, carry):
            v_r, v_i = carry
            for j in range(run):
                at = lanes(start + (i * run + j) * LANES, LANES)
                a_r, a_i = full[pl.ds(0, modes), at], full[pl.ds(modes, modes), at]
                z_r = yz_ref[pl.ds(double, modes), at]
                z_i = yz_ref[pl.ds(double + modes, modes), at]
                v_r = v_r + (a_r * z_r + a_i * z_i)
                v_i = v_i + (a_r * z_i - a_i * z_r)
            return v_r, v_i

        state["cross"] = lax.fori_loop(0, half // (run * LANES), step, state["cross"])

    def fit(p, k):
        start = fit_start(p, k)
        tile = min(FIT_TILE, half)

        def step(i, carry):
            at = lanes(start + i * tile, tile)
            fitted = jnp.dot(
                fit_basis[...],
                full[:, at].astype(jnp.bfloat16),
                preferred_element_type=jnp.float32,
            )
            res_ref[:, at] = (xbuf[:, at].astype(jnp.float32) - fitted).astype(res_ref.dtype)
            return carry

        lax.fori_loop(0, half // tile, step, 0)

    def cross_sum():
        ones = jnp.ones((8, LANES), jnp.float32)
        vsum[0] = jnp.zeros(vsum.shape[1:], jnp.float32)
        vsum[0, :, pl.ds(0, double)] = exact_dot(
            ones, jnp.concatenate(state["cross"], 0), OVER_LANES
        )
        state["v"] = gather_sum_start(vsum.at[0], vnear, near_slot, near, n_send, n_recv)

    def cross_near():
        vsum[1] = gather_sum_end(state["v"], vnear)
        state["v"] = gather_sum_start(vsum.at[1], vfar, far_slot, far, f_send, f_recv)

    invert_jobs = modes // INVERT_STEPS
    script = timeline(orders, tm_bits, width, double, invert_jobs)
    at_sum = script.index(("cross_sum",))
    trailing = [i for i, job in enumerate(script) if i > at_sum and job[0] in ("fit", "hessian")]
    middle = trailing[len(trailing) // 2] if trailing else None
    passed = False
    for i, (name, *where) in enumerate(script):
        if i == middle:
            cross_near()
            passed = True
        if name == "arrive":
            arrive(*where)
        elif name == "rest":
            project(where[0], 1)
        elif name == "gram":
            gram()
        elif name == "invert":
            state["inverse"] = invert_steps(
                *state["inverse"], where[0] * INVERT_STEPS, INVERT_STEPS
            )
            if where[0] == invert_jobs - 1:
                finish_inverse()
        elif name == "hessian":
            state["hessian"] = invert_steps(
                *state["hessian"], where[0] * INVERT_STEPS, INVERT_STEPS
            )
        elif name == "model":
            model()
        elif name == "sum":
            sum_start()
        elif name == "sum_near":
            sum_near()
        elif name == "sum_far":
            sum_far()
        elif name == "cross":
            cross(*where)
        elif name == "fit":
            fit(*where)
        elif name == "cross_sum":
            cross_sum()
    if not passed:
        cross_near()
    v_all = gather_sum_end(state["v"], vfar)[:1]

    wide = (modes, LANES)
    spread = lax.broadcasted_iota(jnp.int32, wide, 1) - lax.broadcasted_iota(jnp.int32, wide, 0)

    def as_column(shift):
        return jnp.sum(jnp.where(spread == shift, v_all, 0.0), 1, keepdims=True)

    grad_r = state["w"][0] - as_column(0)
    grad_i = state["w"][1] - as_column(modes)
    hinv_r, hinv_i = state["hessian"]
    new_ref[pl.ds(0, 1), :] = exps_ref[pl.ds(0, 1), :] - jnp.sum(
        hinv_r * grad_r + hinv_i * grad_i, 0, keepdims=True
    )
    new_ref[pl.ds(1, 1), :] = exps_ref[pl.ds(1, 1), :] - jnp.sum(
        hinv_r * grad_i - hinv_i * grad_r, 0, keepdims=True
    )
    for copy in sends:
        copy.wait_send()


def step(snapshots, exponents, groups, spaces):
    modes = exponents.shape[1]
    double = 2 * modes
    local_rows, columns = snapshots.shape
    tm_bits, sp_bits = groups.bit_length() - 1, spaces.bit_length() - 1
    assert groups == 2**tm_bits and spaces == 2**sp_bits and tm_bits >= 2
    assert 4 * modes == LANES
    parts = min(len(ORDERS), columns // (groups // 2 * LANES))
    width = columns // parts
    low = 2 ** (tm_bits // 2)
    near, far = low * spaces, groups // low
    mid = far // 2

    def buffer(*shape):
        return pltpu.VMEM(shape, jnp.float32)

    def dma(*shape):
        return pltpu.SemaphoreType.DMA(shape)

    vmem = pl.BlockSpec(memory_space=pltpu.VMEM)
    return pl.pallas_call(
        functools.partial(step_kernel, modes, tm_bits, sp_bits, parts),
        out_shape=(
            jax.ShapeDtypeStruct((double, columns), jnp.float32),
            jax.ShapeDtypeStruct(snapshots.shape, snapshots.dtype),
            jax.ShapeDtypeStruct(exponents.shape, jnp.float32),
        ),
        in_specs=[pl.BlockSpec(memory_space=pltpu.HBM), vmem],
        out_specs=(vmem, vmem, vmem),
        scratch_shapes=[
            pltpu.VMEM((local_rows, columns), snapshots.dtype),
            buffer(2 * double, columns),
            pltpu.VMEM((2 * double, local_rows), jnp.bfloat16),
            pltpu.VMEM((local_rows, double), jnp.bfloat16),
            [buffer(parts, double, width >> (s + 1)) for s in range(tm_bits - 1)],
            buffer(parts, double, width >> (tm_bits - 1)),
            buffer(2, modes // 2, LANES),
            buffer(near, modes // 2, LANES),
            buffer(mid, modes // 2, LANES),
            buffer(2, 8, LANES),
            buffer(near, 8, LANES),
            buffer(far, 8, LANES),
            dma(parts, tm_bits), dma(parts, tm_bits),
            dma(parts, tm_bits), dma(parts, tm_bits),
            dma(near - 1), dma(near - 1),
            dma(max(mid - 1, 1)), dma(max(mid - 1, 1)),
            dma(near - 1), dma(near - 1),
            dma(far - 1), dma(far - 1),
            dma(parts, 2),
        ],
        compiler_params=pltpu.CompilerParams(
            collective_id=0, has_side_effects=True, vmem_limit_bytes=40 * 2**20
        ),
    )(snapshots, exponents)


def shards(snapshots, exponents):
    columns = snapshots.shape[1]
    modes = exponents.shape[1]
    groups, spaces = lax.axis_size("tm"), lax.axis_size("space")
    amp_rows, residual, new_exponents = step(snapshots, exponents, groups, spaces)
    return (new_exponents, amp_rows.reshape(2, modes, columns), residual)


def solution(mesh):
    return jax.shard_map(
        shards,
        mesh=mesh,
        in_specs=(P("tm", "space"), P()),
        out_specs=(P(), P(None, None, "space"), P("tm", "space")),
        check_vma=False,
    )
```

```python
import functools
import heapq

import jax
import jax.numpy as jnp
from jax import lax
from jax.experimental import pallas as pl
from jax.experimental.pallas import tpu as pltpu
from jax.sharding import PartitionSpec as P

damping = 0.01
MESH = pl.DeviceIdType.MESH
LANES = 128
TILE = 512
FIT_TILE = 256
INVERT_STEPS = 4
ORDERS = (
    (1, 2, 0), (2, 0, 1), (0, 1, 2), (1, 2, 0), (0, 2, 1), (1, 2, 0), (1, 0, 2), (0, 1, 2),
)
OVER_LANES = ((1,), (1,))

LINK_BYTES_PER_US = 100e3
HOP_US = 2.3
FAR_US = 0.5
STEP_US = 0.15
PROJECT_US = 0.25
AMPLITUDE_US = 0.5
GRAM_US = 1.2
INVERT_US = 0.4
MODEL_US = 1.0
CROSS_US = 0.15
FIT_US = 0.35
START_US = 1.5


def exact_dot(left, right, dims=((1,), (0,))):
    return lax.dot_general(
        left,
        right,
        (dims, ((), ())),
        precision=lax.Precision.HIGHEST,
        preferred_element_type=jnp.float32,
    )


def complex_dot(ar, ai, br, bi):
    return exact_dot(ar, br) - exact_dot(ai, bi), exact_dot(ar, bi) + exact_dot(ai, br)


def complex_product(ar, ai, br, bi):
    return ar * br - ai * bi, ar * bi + ai * br


def invert_steps(real, imag, first, count):
    rows = lax.broadcasted_iota(jnp.int32, real.shape, 0)
    cols = lax.broadcasted_iota(jnp.int32, real.shape, 1)
    for k in range(first, first + count):
        on_row, on_col = rows == k, cols == k
        scale = 1.0 / real[k : k + 1, k : k + 1]
        row_r = jnp.where(on_col[:1], 1.0, real[k : k + 1, :]) * scale
        row_i = jnp.where(on_col[:1], 0.0, imag[k : k + 1, :]) * scale
        col_r, col_i = real[:, k : k + 1], imag[:, k : k + 1]
        real = jnp.where(
            on_row, row_r, jnp.where(on_col, 0.0, real) - (col_r * row_r - col_i * row_i)
        )
        imag = jnp.where(
            on_row, row_i, jnp.where(on_col, 0.0, imag) - (col_r * row_i + col_i * row_r)
        )
    return real, imag


def column_of(row):
    n = row.shape[1]
    here = lax.broadcasted_iota(jnp.int32, (n, n), 0) == lax.broadcasted_iota(
        jnp.int32, (n, n), 1
    )
    return jnp.sum(jnp.where(here, row, 0.0), 1, keepdims=True)


def waves(rate, frequency, time):
    magnitude = jnp.exp(time * rate)
    angle = time * frequency
    return magnitude * jnp.cos(angle), magnitude * jnp.sin(angle)


def moments(real, imag, time):
    modes = real.shape[0]
    both = jnp.concatenate(
        [jnp.concatenate([real, imag], 1), jnp.concatenate([-imag, real], 1)], 0
    )
    first, twice = both[:modes], jnp.concatenate([time, time], 1)
    powers = [first, twice * first, twice * (twice * first)]
    powers += [jnp.zeros_like(first)] * (LANES // modes - len(powers))
    sums = exact_dot(both, jnp.concatenate(powers, 0), OVER_LANES)
    blocks = []
    for n in range(3):
        moved = sums if n == 0 else pltpu.roll(sums, LANES - n * modes, 1)
        blocks.append((moved[:modes, :modes], moved[modes:, :modes]))
    return blocks


def timeline(orders, bits, width, rows, invert_jobs):
    parts, last = len(orders), 2 * bits - 2
    free = {}
    events, script, count = [], [], [0]
    done = set()
    now = START_US

    def post(at, what):
        heapq.heappush(events, (at, count[0], what))
        count[0] += 1

    def send(p, stage):
        s = min(stage, last - stage)
        bit = orders[p][s]
        size = (width >> min(s + 1, bits - 1)) * rows * 4 / LINK_BYTES_PER_US
        delay = HOP_US
        if bit < 2:
            keys = {"xy": size}
        elif bit == 2:
            keys = {"near": 2 * size}
        else:
            keys, delay = {"near": 2 * size, "far": 4 * size}, HOP_US + FAR_US
        start = max([now] + [free.get(k, 0.0) for k in keys])
        for k, v in keys.items():
            free[k] = start + v
        post(start + max(keys.values()) + delay, ("arrive", p, stage))

    for p in range(parts):
        now += PROJECT_US
        send(p, 0)
    jobs = [("rest", p) for p in range(parts)] + [("gram",)]
    jobs += [("invert", i) for i in range(invert_jobs)] + [("model",)]
    cost = {
        "rest": PROJECT_US, "gram": GRAM_US, "invert": INVERT_US, "model": MODEL_US,
        "hessian": INVERT_US, "cross": CROSS_US, "fit": FIT_US,
    }
    rank = {
        "rest": 0, "gram": 1, "invert": 2, "cross": 3, "hessian": 4, "model": 5, "fit": 6,
    }

    def run(job):
        nonlocal now
        jobs.remove(job)
        done.add(job)
        script.append(job)
        now += cost[job[0]]

    amplitudes = crossed = 0
    while events or jobs:
        if events and (events[0][0] <= now or not jobs):
            at, _, what = heapq.heappop(events)
            now = max(now, at)
            if what[0] == "arrive":
                _, p, stage = what
                if stage == 0 and ("rest", p) not in done:
                    run(("rest", p))
                if stage == bits - 1:
                    for job in [j for j in jobs if j[0] in ("gram", "invert")]:
                        run(job)
                    now += AMPLITUDE_US
                    amplitudes += 1
                script.append(what)
                now += STEP_US
                if stage < last:
                    send(p, stage + 1)
                if stage >= last - 1:
                    k = stage - (last - 1)
                    jobs += [("cross", p, k), ("fit", p, k)]
                if amplitudes == parts and ("sum",) not in done:
                    done.add(("sum",))
                    script.append(("sum",))
                    now += AMPLITUDE_US
                    post(now + HOP_US + 1.0, ("sum_near",))
            elif what[0] == "sum_near":
                script.append(what)
                now += STEP_US
                post(now + HOP_US, ("sum_far",))
            else:
                script.append(what)
                if ("model",) in jobs:
                    jobs.remove(("model",))
                    script.insert(len(script) - 1, ("model",))
                jobs += [("hessian", i) for i in range(invert_jobs)]
            continue
        job = min(jobs, key=lambda j: rank[j[0]])
        if events and rank[job[0]] > 2 and events[0][0] < now + 0.05:
            now = events[0][0]
            continue
        run(job)
        if job[0] == "cross":
            crossed += 1
            if crossed == 2 * parts:
                script.append(("cross_sum",))
    return script


def step_kernel(
    modes, tm_bits, sp_bits, parts,
    x_ref, exps_ref,
    full, res_ref, new_ref,
    xbuf, yz_ref, basis, fit_basis, halves, tail, ssum, snear, sfar, vsum, vnear, vfar,
    rs_send, rs_recv, ag_send, ag_recv,
    sn_send, sn_recv, sf_send, sf_recv, n_send, n_recv, f_send, f_recv, x_sem,
):
    double = 2 * modes
    local_rows, columns = xbuf.shape
    width = columns // parts
    half = width // 2
    last = tm_bits - 1
    me, sp = lax.axis_index("tm"), lax.axis_index("space")
    swap = sp % 2

    def stride_of(bit):
        if tm_bits > 2 and bit == 0:
            return 1 + swap
        if tm_bits > 2 and bit == 1:
            return 2 - swap
        return 2**bit

    def flip(index, stride):
        side = (index // stride) % 2
        return side, index + (1 - 2 * side) * stride

    spaces, low = 2**sp_bits, 2 ** (tm_bits // 2)
    n_near, n_far = low * spaces, 2**tm_bits // low
    n_mid = n_far // 2
    near_slot, far_slot = (me % low) * spaces + sp, me // low
    mid_slot = far_slot % n_mid
    near, mid, far = [], [], []
    for d in range(1, n_near):
        other = (near_slot + d) % n_near
        near.append((far_slot * low + other // spaces, other % spaces))
    for d in range(1, n_mid):
        other = (far_slot // n_mid) * n_mid + (mid_slot + d) % n_mid
        mid.append((other * low + me % low, sp))
    for d in range(1, n_far):
        far.append(((far_slot + d) % n_far * low + me % low, sp))

    def lanes(start, size):
        return pl.ds(pl.multiple_of(start, LANES), size)

    orders = []
    for p in range(parts):
        order = [b for b in ORDERS[p % len(ORDERS)] if b < last]
        orders.append(order + [b for b in range(tm_bits) if b not in order])
    plan = [[flip(me, stride_of(b)) for b in order] for order in orders]

    def part_half(p, k):
        side = plan[p][0][0]
        return p * width + ((1 - side) * half if k == 0 else side * half)

    loads = {}
    for k in range(2):
        for p in range(parts):
            at = lanes(part_half(p, k), half)
            loads[p, k] = pltpu.make_async_copy(x_ref.at[:, at], xbuf.at[:, at], x_sem.at[p, k])
            loads[p, k].start()

    barrier = pltpu.get_barrier_semaphore()
    for friend in near + far:
        pl.semaphore_signal(barrier, inc=1, device_id=friend, device_id_type=MESH)

    rate, frequency = column_of(exps_ref[pl.ds(0, 1), :]), column_of(exps_ref[pl.ds(1, 1), :])
    total_rows = local_rows * 2**tm_bits
    steps = lax.broadcasted_iota(jnp.int32, (1, local_rows), 1)
    time = (me * local_rows + steps).astype(jnp.float32) / total_rows
    real, imag = waves(rate, frequency, time)
    plain = jnp.concatenate([real, -imag], 0)
    basis[...] = jnp.concatenate([plain, time * plain], 0).astype(jnp.bfloat16)

    def project(p, k):
        loads[p, k].wait()
        at = part_half(p, k)
        tile = min(TILE, half)

        def step(i, carry):
            here = lanes(at + i * tile, tile)
            yz_ref[:, here] = jnp.dot(
                basis[...], xbuf[:, here], preferred_element_type=jnp.float32
            )
            return carry

        lax.fori_loop(0, half // tile, step, 0)

    sends = []

    def remote(src, dst, send, recv, friend):
        copy = pltpu.make_async_remote_copy(
            src_ref=src, dst_ref=dst, send_sem=send, recv_sem=recv,
            device_id=friend, device_id_type=MESH,
        )
        copy.start()
        sends.append(copy)
        return copy

    flying = {}
    above = pl.ds(0, double)

    def scatter_start(p, s):
        side, partner = plan[p][s]
        size = width >> (s + 1)
        away = (1 - side) * size
        if s == last:
            src, dst = halves[s - 1].at[p], tail.at[p]
        elif s == 0:
            src, dst = yz_ref.at[above, lanes(p * width + away, size)], halves[s].at[p]
        else:
            src, dst = halves[s - 1].at[p, :, lanes(away, size)], halves[s].at[p]
        flying[p] = remote(src, dst, rs_send.at[p, s], rs_recv.at[p, s], (partner, sp))

    def scatter_add(p, s):
        side, _ = plan[p][s]
        size = width >> (s + 1)
        if s == 0:
            mine = yz_ref[above, lanes(p * width + side * size, size)]
        else:
            mine = halves[s - 1][p, :, lanes(side * size, size)]
        halves[s][p] = halves[s][p] + mine

    offsets = []
    for p in range(parts):
        start = p * width
        for s in range(last):
            start = start + plan[p][s][0] * (width >> (s + 1))
        offsets.append(start)

    def gather_start(p, s):
        where = full.at[:, lanes(offsets[p], width >> (s + 1))]
        flying[p] = remote(
            where, where, ag_send.at[p, s], ag_recv.at[p, s], (plan[p][s][1], sp)
        )

    def gather_sum_start(source, landed, slot, peers, send, recv):
        copies = [
            remote(source, landed.at[slot], send.at[d], recv.at[d], peer)
            for d, peer in enumerate(peers)
        ]
        landed[slot] = source[...]
        return copies

    def gather_sum_end(copies, landed):
        for copy in copies:
            copy.wait_recv()
        total = landed[0]
        for k in range(1, len(copies) + 1):
            total = total + landed[k]
        return total

    for p in range(parts):
        project(p, 0)
        if p == 0:
            pl.semaphore_wait(barrier, len(near + far))
        scatter_start(p, 0)

    state = {
        "self": jnp.zeros((double, double), jnp.float32),
        "cross": (jnp.zeros((modes, LANES), jnp.float32),) * 2,
    }
    square = (modes, modes)

    def gram():
        fit_basis[...] = jnp.transpose(plain).astype(jnp.bfloat16)
        base_time = steps.astype(jnp.float32) / total_rows
        base = moments(*waves(rate, frequency, base_time), base_time)
        groups = 2**tm_bits
        wide = max(LANES, groups)
        block = lax.broadcasted_iota(jnp.int32, (1, wide), 1)
        shift_time = (block * local_rows).astype(jnp.float32) / total_rows
        used = block < groups
        shift_time = jnp.where(used, shift_time, 0.0)
        turn_r, turn_i = waves(rate, frequency, shift_time)
        turn = moments(
            jnp.where(used, turn_r, 0.0), jnp.where(used, turn_i, 0.0), shift_time
        )

        def times(m, n):
            return complex_product(*turn[m], *base[n])

        g = times(0, 0)
        c = [a + b for a, b in zip(times(1, 0), times(0, 1))]
        e = [
            a + 2.0 * b + d for a, b, d in zip(times(2, 0), times(1, 1), times(0, 2))
        ]
        state.update(c=c, e=e, inverse=g)

    def finish_inverse():
        inv_r, inv_i = state["inverse"]
        state["solve"] = jnp.concatenate(
            [jnp.concatenate([inv_r, -inv_i], 1), jnp.concatenate([inv_i, inv_r], 1)], 0
        )

    def model():
        c_r, c_i = state["c"]
        t_r, t_i = complex_dot(*state["inverse"], c_r, c_i)
        u_r, u_i = complex_dot(c_r, c_i, t_r, t_i)
        state["m"] = (state["e"][0] - u_r, state["e"][1] - u_i)

    def arrive(p, stage):
        if stage < last:
            flying[p].wait_recv()
            scatter_add(p, stage)
            scatter_start(p, stage + 1)
        elif stage == last:
            flying[p].wait_recv()
            amps = exact_dot(state["solve"], halves[last - 1][p] + tail[p])
            full[:, lanes(offsets[p], width >> last)] = amps
            gather_start(p, last - 1)
            state["self"] = state["self"] + exact_dot(amps, amps, OVER_LANES)
        else:
            s = 2 * last - stage
            flying[p].wait_recv()
            offsets[p] = offsets[p] - plan[p][s][0] * (width >> (s + 1))
            if s > 0:
                gather_start(p, s - 1)

    def sum_start():
        both = state["self"]
        moved = pltpu.roll(jnp.concatenate([both, both], 1), LANES - modes, 1)
        s_r = both[:modes, :modes] + moved[modes:, :modes]
        s_i = moved[:modes, :modes] - both[modes:, :modes]
        pair = jnp.concatenate([s_r, s_i], 1)
        ssum[0] = jnp.concatenate([pair[: modes // 2], pair[modes // 2 :]], 1)
        state["copies"] = gather_sum_start(ssum.at[0], snear, near_slot, near, sn_send, sn_recv)

    def sum_near():
        ssum[1] = gather_sum_end(state["copies"], snear)
        state["copies"] = gather_sum_start(ssum.at[1], sfar, mid_slot, mid, sf_send, sf_recv)

    def sum_far():
        packed = gather_sum_end(state["copies"], sfar)

        def piece(n):
            moved = packed if n == 0 else pltpu.roll(packed, LANES - n * modes, 1)
            return moved[:, :modes]

        s_r = jnp.concatenate([piece(0), piece(2)], 0)
        s_i = jnp.concatenate([piece(1), piece(3)], 0)
        diagonal = lax.broadcasted_iota(jnp.int32, square, 0) == lax.broadcasted_iota(
            jnp.int32, square, 1
        )
        h_r, h_i = complex_product(s_r, s_i, *state["m"])
        c_r, c_i = state["c"]
        state["hessian"] = (h_r + jnp.where(diagonal, damping, 0.0), h_i)
        state["w"] = (
            jnp.sum(c_r * s_r - c_i * s_i, 1, keepdims=True),
            jnp.sum(c_r * s_i + c_i * s_r, 1, keepdims=True),
        )

    def fit_start(p, k):
        return part_half(p, 1 - k)

    def cross(p, k):
        start = fit_start(p, k)
        run = min(4, half // LANES)

        def step(i, carry):
            v_r, v_i = carry
            for j in range(run):
                at = lanes(start + (i * run + j) * LANES, LANES)
                a_r, a_i = full[pl.ds(0, modes), at], full[pl.ds(modes, modes), at]
                z_r = yz_ref[pl.ds(double, modes), at]
                z_i = yz_ref[pl.ds(double + modes, modes), at]
                v_r = v_r + (a_r * z_r + a_i * z_i)
                v_i = v_i + (a_r * z_i - a_i * z_r)
            return v_r, v_i

        state["cross"] = lax.fori_loop(0, half // (run * LANES), step, state["cross"])

    def fit(p, k):
        start = fit_start(p, k)
        tile = min(FIT_TILE, half)

        def step(i, carry):
            at = lanes(start + i * tile, tile)
            fitted = jnp.dot(
                fit_basis[...],
                full[:, at].astype(jnp.bfloat16),
                preferred_element_type=jnp.float32,
            )
            res_ref[:, at] = (xbuf[:, at].astype(jnp.float32) - fitted).astype(res_ref.dtype)
            return carry

        lax.fori_loop(0, half // tile, step, 0)

    def cross_sum():
        ones = jnp.ones((8, LANES), jnp.float32)
        vsum[0] = jnp.zeros(vsum.shape[1:], jnp.float32)
        vsum[0, :, pl.ds(0, double)] = exact_dot(
            ones, jnp.concatenate(state["cross"], 0), OVER_LANES
        )
        state["v"] = gather_sum_start(vsum.at[0], vnear, near_slot, near, n_send, n_recv)

    def cross_near():
        vsum[1] = gather_sum_end(state["v"], vnear)
        state["v"] = gather_sum_start(vsum.at[1], vfar, far_slot, far, f_send, f_recv)

    invert_jobs = modes // INVERT_STEPS
    script = timeline(orders, tm_bits, width, double, invert_jobs)
    at_sum = script.index(("cross_sum",))
    trailing = [i for i, job in enumerate(script) if i > at_sum and job[0] in ("fit", "hessian")]
    middle = trailing[len(trailing) // 2] if trailing else None
    passed = False
    for i, (name, *where) in enumerate(script):
        if i == middle:
            cross_near()
            passed = True
        if name == "arrive":
            arrive(*where)
        elif name == "rest":
            project(where[0], 1)
        elif name == "gram":
            gram()
        elif name == "invert":
            state["inverse"] = invert_steps(
                *state["inverse"], where[0] * INVERT_STEPS, INVERT_STEPS
            )
            if where[0] == invert_jobs - 1:
                finish_inverse()
        elif name == "hessian":
            state["hessian"] = invert_steps(
                *state["hessian"], where[0] * INVERT_STEPS, INVERT_STEPS
            )
        elif name == "model":
            model()
        elif name == "sum":
            sum_start()
        elif name == "sum_near":
            sum_near()
        elif name == "sum_far":
            sum_far()
        elif name == "cross":
            cross(*where)
        elif name == "fit":
            fit(*where)
        elif name == "cross_sum":
            cross_sum()
    if not passed:
        cross_near()
    v_all = gather_sum_end(state["v"], vfar)[:1]

    wide = (modes, LANES)
    spread = lax.broadcasted_iota(jnp.int32, wide, 1) - lax.broadcasted_iota(jnp.int32, wide, 0)

    def as_column(shift):
        return jnp.sum(jnp.where(spread == shift, v_all, 0.0), 1, keepdims=True)

    grad_r = state["w"][0] - as_column(0)
    grad_i = state["w"][1] - as_column(modes)
    hinv_r, hinv_i = state["hessian"]
    new_ref[pl.ds(0, 1), :] = exps_ref[pl.ds(0, 1), :] - jnp.sum(
        hinv_r * grad_r + hinv_i * grad_i, 0, keepdims=True
    )
    new_ref[pl.ds(1, 1), :] = exps_ref[pl.ds(1, 1), :] - jnp.sum(
        hinv_r * grad_i - hinv_i * grad_r, 0, keepdims=True
    )
    for copy in sends:
        copy.wait_send()


def step(snapshots, exponents, groups, spaces):
    modes = exponents.shape[1]
    double = 2 * modes
    local_rows, columns = snapshots.shape
    tm_bits, sp_bits = groups.bit_length() - 1, spaces.bit_length() - 1
    assert groups == 2**tm_bits and spaces == 2**sp_bits and tm_bits >= 2
    assert 4 * modes == LANES
    parts = min(len(ORDERS), columns // (groups // 2 * LANES))
    width = columns // parts
    low = 2 ** (tm_bits // 2)
    near, far = low * spaces, groups // low
    mid = far // 2

    def buffer(*shape):
        return pltpu.VMEM(shape, jnp.float32)

    def dma(*shape):
        return pltpu.SemaphoreType.DMA(shape)

    vmem = pl.BlockSpec(memory_space=pltpu.VMEM)
    return pl.pallas_call(
        functools.partial(step_kernel, modes, tm_bits, sp_bits, parts),
        out_shape=(
            jax.ShapeDtypeStruct((double, columns), jnp.float32),
            jax.ShapeDtypeStruct(snapshots.shape, snapshots.dtype),
            jax.ShapeDtypeStruct(exponents.shape, jnp.float32),
        ),
        in_specs=[pl.BlockSpec(memory_space=pltpu.HBM), vmem],
        out_specs=(vmem, vmem, vmem),
        scratch_shapes=[
            pltpu.VMEM((local_rows, columns), snapshots.dtype),
            buffer(2 * double, columns),
            pltpu.VMEM((2 * double, local_rows), jnp.bfloat16),
            pltpu.VMEM((local_rows, double), jnp.bfloat16),
            [buffer(parts, double, width >> (s + 1)) for s in range(tm_bits - 1)],
            buffer(parts, double, width >> (tm_bits - 1)),
            buffer(2, modes // 2, LANES),
            buffer(near, modes // 2, LANES),
            buffer(mid, modes // 2, LANES),
            buffer(2, 8, LANES),
            buffer(near, 8, LANES),
            buffer(far, 8, LANES),
            dma(parts, tm_bits), dma(parts, tm_bits),
            dma(parts, tm_bits), dma(parts, tm_bits),
            dma(near - 1), dma(near - 1),
            dma(max(mid - 1, 1)), dma(max(mid - 1, 1)),
            dma(near - 1), dma(near - 1),
            dma(far - 1), dma(far - 1),
            dma(parts, 2),
        ],
        compiler_params=pltpu.CompilerParams(
            collective_id=0, has_side_effects=True, vmem_limit_bytes=40 * 2**20
        ),
    )(snapshots, exponents)


def write_kernel(pieces, *refs):
    sources, targets, sem = refs[:3], refs[3:6], refs[6]
    copies = []
    for i, (source, target) in enumerate(zip(sources, targets)):
        rows = source.shape[0] // pieces[i]
        for j in range(pieces[i]):
            part = pl.ds(j * rows, rows)
            copies.append((source.at[part], target.at[part]))
    copies = [
        pltpu.make_async_copy(source, target, sem.at[i])
        for i, (source, target) in enumerate(copies)
    ]
    for copy in copies:
        copy.start()
    for copy in copies:
        copy.wait()


def write(residual, amp_rows, new_exponents):
    pieces = (8, 2, 1)
    arrays = (residual, amp_rows, new_exponents)
    return pl.pallas_call(
        functools.partial(write_kernel, pieces),
        out_shape=tuple(jax.ShapeDtypeStruct(a.shape, a.dtype) for a in arrays),
        in_specs=[pl.BlockSpec(memory_space=pltpu.VMEM)] * 3,
        out_specs=[pl.BlockSpec(memory_space=pltpu.HBM)] * 3,
        scratch_shapes=[pltpu.SemaphoreType.DMA((sum(pieces),))],
        compiler_params=pltpu.CompilerParams(vmem_limit_bytes=24 * 2**20),
    )(*arrays)


def shards(snapshots, exponents):
    columns = snapshots.shape[1]
    modes = exponents.shape[1]
    groups, spaces = lax.axis_size("tm"), lax.axis_size("space")
    amp_rows, residual, new_exponents = step(snapshots, exponents, groups, spaces)
    residual, amp_rows, new_exponents = write(residual, amp_rows, new_exponents)
    return (new_exponents, amp_rows.reshape(2, modes, columns), residual)


def solution(mesh):
    return jax.shard_map(
        shards,
        mesh=mesh,
        in_specs=(P("tm", "space"), P()),
        out_specs=(P(), P(None, None, "space"), P("tm", "space")),
        check_vma=False,
    )
```

```python
import functools
import heapq

import jax
import jax.numpy as jnp
from jax import lax
from jax.experimental import pallas as pl
from jax.experimental.pallas import tpu as pltpu
from jax.sharding import PartitionSpec as P

damping = 0.01
MESH = pl.DeviceIdType.MESH
LANES = 128
TILE = 512
FIT_TILE = 256
INVERT_STEPS = 4
ORDERS = (
    (1, 0, 3, 2), (3, 0, 2, 1), (0, 2, 1, 3), (0, 2, 1, 3),
    (1, 3, 0, 2), (1, 2, 0, 3), (2, 1, 0, 3), (0, 1, 2, 3),
)
ONE_STEP_DEVICES = 32
OVER_LANES = ((1,), (1,))

LINK_BYTES_PER_US = 100e3
HOP_US = 2.45
FAR_US = 0.42
STEP_US = 0.12
PROJECT_US = 0.25
AMPLITUDE_US = 0.45
GRAM_US = 1.0
INVERT_US = 0.35
MODEL_US = 0.6
CROSS_US = 0.05
FIT_US = 0.45
START_US = 1.7


def exact_dot(left, right, dims=((1,), (0,))):
    return lax.dot_general(
        left,
        right,
        (dims, ((), ())),
        precision=lax.Precision.HIGHEST,
        preferred_element_type=jnp.float32,
    )


def complex_dot(ar, ai, br, bi):
    return exact_dot(ar, br) - exact_dot(ai, bi), exact_dot(ar, bi) + exact_dot(ai, br)


def complex_product(ar, ai, br, bi):
    return ar * br - ai * bi, ar * bi + ai * br


def invert_steps(real, imag, first, count):
    rows = lax.broadcasted_iota(jnp.int32, real.shape, 0)
    cols = lax.broadcasted_iota(jnp.int32, real.shape, 1)
    for k in range(first, first + count):
        on_row, on_col = rows == k, cols == k
        scale = 1.0 / real[k : k + 1, k : k + 1]
        row_r = jnp.where(on_col[:1], 1.0, real[k : k + 1, :]) * scale
        row_i = jnp.where(on_col[:1], 0.0, imag[k : k + 1, :]) * scale
        col_r, col_i = real[:, k : k + 1], imag[:, k : k + 1]
        real = jnp.where(
            on_row, row_r, jnp.where(on_col, 0.0, real) - (col_r * row_r - col_i * row_i)
        )
        imag = jnp.where(
            on_row, row_i, jnp.where(on_col, 0.0, imag) - (col_r * row_i + col_i * row_r)
        )
    return real, imag


def column_of(row):
    n = row.shape[1]
    here = lax.broadcasted_iota(jnp.int32, (n, n), 0) == lax.broadcasted_iota(
        jnp.int32, (n, n), 1
    )
    return jnp.sum(jnp.where(here, row, 0.0), 1, keepdims=True)


def waves(rate, frequency, time):
    magnitude = jnp.exp(time * rate)
    angle = time * frequency
    return magnitude * jnp.cos(angle), magnitude * jnp.sin(angle)


def moments(real, imag, time):
    modes = real.shape[0]
    both = jnp.concatenate(
        [jnp.concatenate([real, imag], 1), jnp.concatenate([-imag, real], 1)], 0
    )
    first, twice = both[:modes], jnp.concatenate([time, time], 1)
    powers = [first, twice * first, twice * (twice * first)]
    powers += [jnp.zeros_like(first)] * (LANES // modes - len(powers))
    sums = exact_dot(both, jnp.concatenate(powers, 0), OVER_LANES)
    blocks = []
    for n in range(3):
        moved = sums if n == 0 else pltpu.roll(sums, LANES - n * modes, 1)
        blocks.append((moved[:modes, :modes], moved[modes:, :modes]))
    return blocks


def timeline(orders, bits, width, rows, invert_jobs):
    parts, last = len(orders), 2 * bits - 2
    free = {}
    events, script, count = [], [], [0]
    done = set()
    now = START_US

    def post(at, what):
        heapq.heappush(events, (at, count[0], what))
        count[0] += 1

    def send(p, stage):
        s = min(stage, last - stage)
        bit = orders[p][s]
        size = (width >> min(s + 1, bits - 1)) * rows * 4 / LINK_BYTES_PER_US
        delay = HOP_US
        if bit < 2:
            keys = {"xy": size}
        elif bit == 2:
            keys = {"near": 2 * size}
        else:
            keys, delay = {"near": 2 * size, "far": 4 * size}, HOP_US + FAR_US
        start = max([now] + [free.get(k, 0.0) for k in keys])
        for k, v in keys.items():
            free[k] = start + v
        post(start + max(keys.values()) + delay, ("arrive", p, stage))

    for p in range(parts):
        now += PROJECT_US
        send(p, 0)
    jobs = [("rest", p) for p in range(parts)] + [("gram",)]
    jobs += [("invert", i) for i in range(invert_jobs)] + [("model",)]
    cost = {
        "rest": PROJECT_US, "gram": GRAM_US, "invert": INVERT_US, "model": MODEL_US,
        "hessian": INVERT_US, "cross": CROSS_US, "fit": FIT_US,
    }
    rank = {
        "rest": 0, "gram": 1, "invert": 2, "cross": 3, "hessian": 4, "model": 5, "fit": 6,
    }

    def run(job):
        nonlocal now
        jobs.remove(job)
        done.add(job)
        script.append(job)
        now += cost[job[0]]

    amplitudes = crossed = 0
    while events or jobs:
        if events and (events[0][0] <= now or not jobs):
            at, _, what = heapq.heappop(events)
            now = max(now, at)
            if what[0] == "arrive":
                _, p, stage = what
                if stage == 0 and ("rest", p) not in done:
                    run(("rest", p))
                if stage == bits - 1:
                    for job in [j for j in jobs if j[0] in ("gram", "invert")]:
                        run(job)
                    now += AMPLITUDE_US
                    amplitudes += 1
                script.append(what)
                now += STEP_US
                if stage < last:
                    send(p, stage + 1)
                if stage >= last - 1:
                    k = stage - (last - 1)
                    jobs += [("cross", p, k), ("fit", p, k)]
                if amplitudes == parts and ("sum",) not in done:
                    done.add(("sum",))
                    script.append(("sum",))
                    now += AMPLITUDE_US
                    post(max([now, *free.values()]) + HOP_US + 1.0, ("sum_near",))
            elif what[0] == "sum_near":
                script.append(what)
                now += STEP_US
                post(max([now, *free.values()]) + HOP_US + 1.5, ("sum_far",))
            else:
                script.append(what)
                if ("model",) in jobs:
                    jobs.remove(("model",))
                    script.insert(len(script) - 1, ("model",))
                jobs += [("hessian", i) for i in range(invert_jobs)]
            continue
        job = min(jobs, key=lambda j: rank[j[0]])
        if events and rank[job[0]] > 2 and events[0][0] < now + 0.05:
            now = events[0][0]
            continue
        run(job)
        if job[0] == "cross":
            crossed += 1
            if crossed == 2 * parts:
                script.append(("cross_sum",))
    return script


def step_kernel(
    modes, tm_bits, sp_bits, parts,
    x_ref, exps_in,
    full, res_ref, new_ref,
    exps_ref, xbuf, yz_ref, basis, fit_basis, halves, tail, ssum, snear, sfar, vsum, vnear, vfar,
    rs_send, rs_recv, ag_send, ag_recv,
    sn_send, sn_recv, sf_send, sf_recv, n_send, n_recv, f_send, f_recv, x_sem, exps_sem,
):
    double = 2 * modes
    local_rows, columns = xbuf.shape
    width = columns // parts
    half = width // 2
    last = tm_bits - 1
    me, sp = lax.axis_index("tm"), lax.axis_index("space")
    swap = sp % 2

    def stride_of(bit):
        if tm_bits > 2 and bit == 0:
            return 1 + swap
        if tm_bits > 2 and bit == 1:
            return 2 - swap
        return 2**bit

    def flip(index, stride):
        side = (index // stride) % 2
        return side, index + (1 - 2 * side) * stride

    spaces, low = 2**sp_bits, 2 ** (tm_bits // 2)
    n_near, n_far = low * spaces, 2**tm_bits // low
    near_slot, far_slot = (me % low) * spaces + sp, me // low
    near, far = [], []
    for d in range(1, n_near):
        other = (near_slot + d) % n_near
        near.append((far_slot * low + other // spaces, other % spaces))
    for d in range(1, n_far):
        far.append(((far_slot + d) % n_far * low + me % low, sp))
    n_all = 2**tm_bits * spaces
    every, every_slot = [], me * spaces + sp
    for d in range(1, n_all):
        other = (every_slot + d) % n_all
        every.append((other // spaces, other % spaces))
    one_step = len(every) < ONE_STEP_DEVICES
    friends = every if one_step else near + far

    def lanes(start, size):
        return pl.ds(pl.multiple_of(start, LANES), size)

    orders = []
    for p in range(parts):
        order = [b for b in ORDERS[p % len(ORDERS)] if b < tm_bits]
        orders.append([b for b in range(tm_bits) if b not in order] + order)
    plan = [[flip(me, stride_of(b)) for b in order] for order in orders]

    def part_half(p, k):
        side = plan[p][0][0]
        return p * width + ((1 - side) * half if k == 0 else side * half)

    exps_load = pltpu.make_async_copy(exps_in, exps_ref, exps_sem)
    exps_load.start()
    loads = {}
    for k in range(2):
        for p in range(parts):
            at = lanes(part_half(p, k), half)
            loads[p, k] = pltpu.make_async_copy(x_ref.at[:, at], xbuf.at[:, at], x_sem.at[p, k])
            loads[p, k].start()

    barrier = pltpu.get_barrier_semaphore()
    for friend in friends:
        pl.semaphore_signal(barrier, inc=1, device_id=friend, device_id_type=MESH)

    exps_load.wait()
    rate, frequency = column_of(exps_ref[pl.ds(0, 1), :]), column_of(exps_ref[pl.ds(1, 1), :])
    total_rows = local_rows * 2**tm_bits
    steps = lax.broadcasted_iota(jnp.int32, (1, local_rows), 1)
    time = (me * local_rows + steps).astype(jnp.float32) / total_rows
    real, imag = waves(rate, frequency, time)
    plain = jnp.concatenate([real, -imag], 0)
    basis[...] = jnp.concatenate([plain, time * plain], 0).astype(jnp.bfloat16)

    def project(p, k):
        loads[p, k].wait()
        at = part_half(p, k)
        tile = min(TILE, half)

        def step(i, carry):
            here = lanes(at + i * tile, tile)
            yz_ref[:, here] = jnp.dot(
                basis[...], xbuf[:, here], preferred_element_type=jnp.float32
            )
            return carry

        lax.fori_loop(0, half // tile, step, 0)

    sends = []

    def remote(src, dst, send, recv, friend):
        copy = pltpu.make_async_remote_copy(
            src_ref=src, dst_ref=dst, send_sem=send, recv_sem=recv,
            device_id=friend, device_id_type=MESH,
        )
        copy.start()
        sends.append(copy)
        return copy

    flying = {}
    above = pl.ds(0, double)

    def scatter_start(p, s):
        side, partner = plan[p][s]
        size = width >> (s + 1)
        away = (1 - side) * size
        if s == last:
            src, dst = halves[s - 1].at[p], tail.at[p]
        elif s == 0:
            src, dst = yz_ref.at[above, lanes(p * width + away, size)], halves[s].at[p]
        else:
            src, dst = halves[s - 1].at[p, :, lanes(away, size)], halves[s].at[p]
        flying[p] = remote(src, dst, rs_send.at[p, s], rs_recv.at[p, s], (partner, sp))

    def scatter_add(p, s):
        side, _ = plan[p][s]
        size = width >> (s + 1)
        if s == 0:
            mine = yz_ref[above, lanes(p * width + side * size, size)]
        else:
            mine = halves[s - 1][p, :, lanes(side * size, size)]
        halves[s][p] = halves[s][p] + mine

    offsets = []
    for p in range(parts):
        start = p * width
        for s in range(last):
            start = start + plan[p][s][0] * (width >> (s + 1))
        offsets.append(start)

    def gather_start(p, s):
        where = full.at[:, lanes(offsets[p], width >> (s + 1))]
        flying[p] = remote(
            where, where, ag_send.at[p, s], ag_recv.at[p, s], (plan[p][s][1], sp)
        )

    def gather_sum_start(source, landed, slot, peers, send, recv):
        copies = [
            remote(source, landed.at[slot], send.at[d], recv.at[d], peer)
            for d, peer in enumerate(peers)
        ]
        landed[slot] = source[...]
        return copies

    def gather_sum_end(copies, landed):
        for copy in copies:
            copy.wait_recv()
        total = landed[0]
        for k in range(1, len(copies) + 1):
            total = total + landed[k]
        return total

    for p in range(parts):
        project(p, 0)
        if p == 0:
            pl.semaphore_wait(barrier, len(friends))
        scatter_start(p, 0)

    state = {
        "self": jnp.zeros((double, double), jnp.float32),
        "cross": (jnp.zeros((modes, LANES), jnp.float32),) * 2,
    }
    square = (modes, modes)

    def gram():
        fit_basis[...] = jnp.transpose(plain).astype(jnp.bfloat16)
        base_time = steps.astype(jnp.float32) / total_rows
        base = moments(*waves(rate, frequency, base_time), base_time)
        groups = 2**tm_bits
        wide = max(LANES, groups)
        block = lax.broadcasted_iota(jnp.int32, (1, wide), 1)
        shift_time = (block * local_rows).astype(jnp.float32) / total_rows
        used = block < groups
        shift_time = jnp.where(used, shift_time, 0.0)
        turn_r, turn_i = waves(rate, frequency, shift_time)
        turn = moments(
            jnp.where(used, turn_r, 0.0), jnp.where(used, turn_i, 0.0), shift_time
        )

        def times(m, n):
            return complex_product(*turn[m], *base[n])

        g = times(0, 0)
        c = [a + b for a, b in zip(times(1, 0), times(0, 1))]
        e = [
            a + 2.0 * b + d for a, b, d in zip(times(2, 0), times(1, 1), times(0, 2))
        ]
        state.update(c=c, e=e, inverse=g)

    def finish_inverse():
        inv_r, inv_i = state["inverse"]
        state["solve"] = jnp.concatenate(
            [jnp.concatenate([inv_r, -inv_i], 1), jnp.concatenate([inv_i, inv_r], 1)], 0
        )

    def model():
        c_r, c_i = state["c"]
        t_r, t_i = complex_dot(*state["inverse"], c_r, c_i)
        u_r, u_i = complex_dot(c_r, c_i, t_r, t_i)
        state["m"] = (state["e"][0] - u_r, state["e"][1] - u_i)

    def arrive(p, stage):
        if stage < last:
            flying[p].wait_recv()
            scatter_add(p, stage)
            scatter_start(p, stage + 1)
        elif stage == last:
            flying[p].wait_recv()
            amps = exact_dot(state["solve"], halves[last - 1][p] + tail[p])
            full[:, lanes(offsets[p], width >> last)] = amps
            gather_start(p, last - 1)
            state["self"] = state["self"] + exact_dot(amps, amps, OVER_LANES)
        else:
            s = 2 * last - stage
            flying[p].wait_recv()
            offsets[p] = offsets[p] - plan[p][s][0] * (width >> (s + 1))
            if s > 0:
                gather_start(p, s - 1)

    def sum_start():
        both = state["self"]
        moved = pltpu.roll(jnp.concatenate([both, both], 1), LANES - modes, 1)
        s_r = both[:modes, :modes] + moved[modes:, :modes]
        s_i = moved[:modes, :modes] - both[modes:, :modes]
        pair = 0.5 * jnp.concatenate([s_r, s_i], 1)
        ssum[0] = jnp.concatenate([pair[: modes // 2], pair[modes // 2 :]], 1)
        state["copies"] = gather_sum_start(ssum.at[0], snear, near_slot, near, sn_send, sn_recv)

    def sum_near():
        ssum[1] = gather_sum_end(state["copies"], snear)
        state["copies"] = gather_sum_start(ssum.at[1], sfar, far_slot, far, sf_send, sf_recv)

    def sum_far():
        packed = gather_sum_end(state["copies"], sfar)

        def piece(n):
            moved = packed if n == 0 else pltpu.roll(packed, LANES - n * modes, 1)
            return moved[:, :modes]

        s_r = jnp.concatenate([piece(0), piece(2)], 0)
        s_i = jnp.concatenate([piece(1), piece(3)], 0)
        diagonal = lax.broadcasted_iota(jnp.int32, square, 0) == lax.broadcasted_iota(
            jnp.int32, square, 1
        )
        h_r, h_i = complex_product(s_r, s_i, *state["m"])
        c_r, c_i = state["c"]
        state["hessian"] = (h_r + jnp.where(diagonal, damping, 0.0), h_i)
        state["w"] = (
            jnp.sum(c_r * s_r - c_i * s_i, 1, keepdims=True),
            jnp.sum(c_r * s_i + c_i * s_r, 1, keepdims=True),
        )

    def fit_start(p, k):
        return part_half(p, 1 - k)

    def cross(p, k):
        start = fit_start(p, k)
        run = min(4, half // LANES)

        def step(i, carry):
            v_r, v_i = carry
            for j in range(run):
                at = lanes(start + (i * run + j) * LANES, LANES)
                a_r, a_i = full[pl.ds(0, modes), at], full[pl.ds(modes, modes), at]
                z_r = yz_ref[pl.ds(double, modes), at]
                z_i = yz_ref[pl.ds(double + modes, modes), at]
                v_r = v_r + (a_r * z_r + a_i * z_i)
                v_i = v_i + (a_r * z_i - a_i * z_r)
            return v_r, v_i

        state["cross"] = lax.fori_loop(0, half // (run * LANES), step, state["cross"])

    def fit(p, k):
        start = fit_start(p, k)
        tile = min(FIT_TILE, half)

        def step(i, carry):
            at = lanes(start + i * tile, tile)
            fitted = jnp.dot(
                fit_basis[...],
                full[:, at].astype(jnp.bfloat16),
                preferred_element_type=jnp.float32,
            )
            res_ref[:, at] = (xbuf[:, at].astype(jnp.float32) - fitted).astype(res_ref.dtype)
            return carry

        lax.fori_loop(0, half // tile, step, 0)

    def cross_sum():
        ones = jnp.ones((8, LANES), jnp.float32)
        vsum[0] = jnp.zeros(vsum.shape[1:], jnp.float32)
        vsum[0, :, pl.ds(0, double)] = exact_dot(
            ones, jnp.concatenate(state["cross"], 0), OVER_LANES
        )
        slot, peers = (every_slot, every) if one_step else (near_slot, near)
        state["v"] = gather_sum_start(vsum.at[0], vnear, slot, peers, n_send, n_recv)

    def cross_near():
        if not one_step:
            vsum[1] = gather_sum_end(state["v"], vnear)
            state["v"] = gather_sum_start(vsum.at[1], vfar, far_slot, far, f_send, f_recv)

    invert_jobs = modes // INVERT_STEPS
    script = timeline(orders, tm_bits, width, double, invert_jobs)
    at_sum = script.index(("cross_sum",))
    trailing = [i for i, job in enumerate(script) if i > at_sum and job[0] in ("fit", "hessian")]
    middle = trailing[len(trailing) // 2] if trailing else None
    passed = False
    for i, (name, *where) in enumerate(script):
        if i == middle:
            cross_near()
            passed = True
        if name == "arrive":
            arrive(*where)
        elif name == "rest":
            project(where[0], 1)
        elif name == "gram":
            gram()
        elif name == "invert":
            state["inverse"] = invert_steps(
                *state["inverse"], where[0] * INVERT_STEPS, INVERT_STEPS
            )
            if where[0] == invert_jobs - 1:
                finish_inverse()
        elif name == "hessian":
            state["hessian"] = invert_steps(
                *state["hessian"], where[0] * INVERT_STEPS, INVERT_STEPS
            )
        elif name == "model":
            model()
        elif name == "sum":
            sum_start()
        elif name == "sum_near":
            sum_near()
        elif name == "sum_far":
            sum_far()
        elif name == "cross":
            cross(*where)
        elif name == "fit":
            fit(*where)
        elif name == "cross_sum":
            cross_sum()
    if not passed:
        cross_near()
    for copy in sends:
        copy.wait_send()
    v_all = gather_sum_end(state["v"], vnear if one_step else vfar)[:1]

    wide = (modes, LANES)
    spread = lax.broadcasted_iota(jnp.int32, wide, 1) - lax.broadcasted_iota(jnp.int32, wide, 0)

    def as_column(shift):
        return jnp.sum(jnp.where(spread == shift, v_all, 0.0), 1, keepdims=True)

    grad_r = state["w"][0] - as_column(0)
    grad_i = state["w"][1] - as_column(modes)
    hinv_r, hinv_i = state["hessian"]
    new_ref[pl.ds(0, 1), :] = exps_ref[pl.ds(0, 1), :] - jnp.sum(
        hinv_r * grad_r + hinv_i * grad_i, 0, keepdims=True
    )
    new_ref[pl.ds(1, 1), :] = exps_ref[pl.ds(1, 1), :] - jnp.sum(
        hinv_r * grad_i - hinv_i * grad_r, 0, keepdims=True
    )


def step(snapshots, exponents, groups, spaces):
    modes = exponents.shape[1]
    double = 2 * modes
    local_rows, columns = snapshots.shape
    tm_bits, sp_bits = groups.bit_length() - 1, spaces.bit_length() - 1
    assert groups == 2**tm_bits and spaces == 2**sp_bits and tm_bits >= 2
    assert 4 * modes == LANES
    parts = min(len(ORDERS), columns // (groups // 2 * LANES))
    width = columns // parts
    low = 2 ** (tm_bits // 2)
    near, far = low * spaces, groups // low
    every = groups * spaces
    v_near = every if every <= ONE_STEP_DEVICES else near

    def buffer(*shape):
        return pltpu.VMEM(shape, jnp.float32)

    def dma(*shape):
        return pltpu.SemaphoreType.DMA(shape)

    vmem = pl.BlockSpec(memory_space=pltpu.VMEM)
    return pl.pallas_call(
        functools.partial(step_kernel, modes, tm_bits, sp_bits, parts),
        out_shape=(
            jax.ShapeDtypeStruct((double, columns), jnp.float32),
            jax.ShapeDtypeStruct(snapshots.shape, snapshots.dtype),
            jax.ShapeDtypeStruct(exponents.shape, jnp.float32),
        ),
        in_specs=[pl.BlockSpec(memory_space=pltpu.HBM)] * 2,
        out_specs=(vmem, vmem, vmem),
        scratch_shapes=[
            buffer(*exponents.shape),
            pltpu.VMEM((local_rows, columns), snapshots.dtype),
            buffer(2 * double, columns),
            pltpu.VMEM((2 * double, local_rows), jnp.bfloat16),
            pltpu.VMEM((local_rows, double), jnp.bfloat16),
            [buffer(parts, double, width >> (s + 1)) for s in range(tm_bits - 1)],
            buffer(parts, double, width >> (tm_bits - 1)),
            buffer(2, modes // 2, LANES),
            buffer(near, modes // 2, LANES),
            buffer(far, modes // 2, LANES),
            buffer(2, 8, LANES),
            buffer(v_near, 8, LANES),
            buffer(far, 8, LANES),
            dma(parts, tm_bits), dma(parts, tm_bits),
            dma(parts, tm_bits), dma(parts, tm_bits),
            dma(near - 1), dma(near - 1),
            dma(far - 1), dma(far - 1),
            dma(v_near - 1), dma(v_near - 1),
            dma(far - 1), dma(far - 1),
            dma(parts, 2),
            pltpu.SemaphoreType.DMA,
        ],
        compiler_params=pltpu.CompilerParams(
            collective_id=0, has_side_effects=True, vmem_limit_bytes=40 * 2**20
        ),
    )(snapshots, exponents)


def write_kernel(pieces, *refs):
    sources, targets, sem = refs[:3], refs[3:6], refs[6]
    copies = []
    for i, (source, target) in enumerate(zip(sources, targets)):
        rows = source.shape[0] // pieces[i]
        for j in range(pieces[i]):
            part = pl.ds(j * rows, rows)
            copies.append((source.at[part], target.at[part]))
    copies = [
        pltpu.make_async_copy(source, target, sem.at[i])
        for i, (source, target) in enumerate(copies)
    ]
    for copy in copies:
        copy.start()
    for copy in copies:
        copy.wait()


def write(residual, amp_rows, new_exponents):
    pieces = (8, 2, 1)
    arrays = (residual, amp_rows, new_exponents)
    return pl.pallas_call(
        functools.partial(write_kernel, pieces),
        out_shape=tuple(jax.ShapeDtypeStruct(a.shape, a.dtype) for a in arrays),
        in_specs=[pl.BlockSpec(memory_space=pltpu.VMEM)] * 3,
        out_specs=[pl.BlockSpec(memory_space=pltpu.HBM)] * 3,
        scratch_shapes=[pltpu.SemaphoreType.DMA((sum(pieces),))],
        compiler_params=pltpu.CompilerParams(vmem_limit_bytes=24 * 2**20),
    )(*arrays)


def shards(snapshots, exponents):
    columns = snapshots.shape[1]
    modes = exponents.shape[1]
    groups, spaces = lax.axis_size("tm"), lax.axis_size("space")
    amp_rows, residual, new_exponents = step(snapshots, exponents, groups, spaces)
    residual, amp_rows, new_exponents = write(residual, amp_rows, new_exponents)
    return (new_exponents, amp_rows.reshape(2, modes, columns), residual)


def solution(mesh):
    return jax.shard_map(
        shards,
        mesh=mesh,
        in_specs=(P("tm", "space"), P()),
        out_specs=(P(), P(None, None, "space"), P("tm", "space")),
        check_vma=False,
    )
```

```python
import functools
import heapq

import jax
import jax.numpy as jnp
from jax import lax
from jax.experimental import pallas as pl
from jax.experimental.pallas import tpu as pltpu
from jax.sharding import PartitionSpec as P

damping = 0.01
MESH = pl.DeviceIdType.MESH
LANES = 128
TILE = 512
FIT_TILE = 256
INVERT_STEPS = 2
ORDERS = (
    (3, 0, 2, 1), (0, 2, 1, 3), (0, 1, 2, 3), (1, 0, 3, 2), (0, 1, 3, 2), (2, 0, 1, 3), (2, 0, 1, 3), (0, 1, 2, 3),
)
ONE_STEP_DEVICES = 32
OVER_LANES = ((1,), (1,))

LINK_BYTES_PER_US = 100e3
HOP_US = 2.45
FAR_US = 0.42
STEP_US = 0.12
PROJECT_US = 0.25
AMPLITUDE_US = 0.45
GRAM_US = 1.0
INVERT_US = 0.18
MODEL_US = 0.6
CROSS_US = 0.05
FIT_US = 0.23
SLACK_US = 0.1
START_US = 1.7


def exact_dot(left, right, dims=((1,), (0,))):
    return lax.dot_general(
        left,
        right,
        (dims, ((), ())),
        precision=lax.Precision.HIGHEST,
        preferred_element_type=jnp.float32,
    )


def complex_dot(ar, ai, br, bi):
    return exact_dot(ar, br) - exact_dot(ai, bi), exact_dot(ar, bi) + exact_dot(ai, br)


def complex_product(ar, ai, br, bi):
    return ar * br - ai * bi, ar * bi + ai * br


def invert_steps(real, imag, first, count):
    rows = lax.broadcasted_iota(jnp.int32, real.shape, 0)
    cols = lax.broadcasted_iota(jnp.int32, real.shape, 1)
    for k in range(first, first + count):
        on_row, on_col = rows == k, cols == k
        scale = 1.0 / real[k : k + 1, k : k + 1]
        row_r = jnp.where(on_col[:1], 1.0, real[k : k + 1, :]) * scale
        row_i = jnp.where(on_col[:1], 0.0, imag[k : k + 1, :]) * scale
        col_r, col_i = real[:, k : k + 1], imag[:, k : k + 1]
        real = jnp.where(
            on_row, row_r, jnp.where(on_col, 0.0, real) - (col_r * row_r - col_i * row_i)
        )
        imag = jnp.where(
            on_row, row_i, jnp.where(on_col, 0.0, imag) - (col_r * row_i + col_i * row_r)
        )
    return real, imag


def column_of(row):
    n = row.shape[1]
    here = lax.broadcasted_iota(jnp.int32, (n, n), 0) == lax.broadcasted_iota(
        jnp.int32, (n, n), 1
    )
    return jnp.sum(jnp.where(here, row, 0.0), 1, keepdims=True)


def waves(rate, frequency, time):
    magnitude = jnp.exp(time * rate)
    angle = time * frequency
    return magnitude * jnp.cos(angle), magnitude * jnp.sin(angle)


def moments(real, imag, time):
    modes = real.shape[0]
    both = jnp.concatenate(
        [jnp.concatenate([real, imag], 1), jnp.concatenate([-imag, real], 1)], 0
    )
    first, twice = both[:modes], jnp.concatenate([time, time], 1)
    powers = [first, twice * first, twice * (twice * first)]
    powers += [jnp.zeros_like(first)] * (LANES // modes - len(powers))
    sums = exact_dot(both, jnp.concatenate(powers, 0), OVER_LANES)
    blocks = []
    for n in range(3):
        moved = sums if n == 0 else pltpu.roll(sums, LANES - n * modes, 1)
        blocks.append((moved[:modes, :modes], moved[modes:, :modes]))
    return blocks


def timeline(orders, bits, width, rows, invert_jobs, fit_jobs):
    parts, last = len(orders), 2 * bits - 2
    free = {}
    events, script, count = [], [], [0]
    done = set()
    now = START_US

    def post(at, what):
        heapq.heappush(events, (at, count[0], what))
        count[0] += 1

    def send(p, stage):
        s = min(stage, last - stage)
        bit = orders[p][s]
        size = (width >> min(s + 1, bits - 1)) * rows * 4 / LINK_BYTES_PER_US
        delay = HOP_US
        if bit < 2:
            keys = {"xy": size}
        elif bit == 2:
            keys = {"near": 2 * size}
        else:
            keys, delay = {"near": 2 * size, "far": 4 * size}, HOP_US + FAR_US
        start = max([now] + [free.get(k, 0.0) for k in keys])
        for k, v in keys.items():
            free[k] = start + v
        post(start + max(keys.values()) + delay, ("arrive", p, stage))

    for p in range(parts):
        now += PROJECT_US
        send(p, 0)
    jobs = [("rest", p) for p in range(parts)] + [("gram",)]
    jobs += [("invert", i) for i in range(invert_jobs)] + [("model",)]
    cost = {
        "rest": PROJECT_US, "gram": GRAM_US, "invert": INVERT_US, "model": MODEL_US,
        "hessian": INVERT_US, "cross": CROSS_US, "fit": FIT_US,
    }
    rank = {
        "rest": 0, "gram": 1, "invert": 2, "cross": 3, "hessian": 4, "model": 5, "fit": 6,
    }

    def run(job):
        nonlocal now
        jobs.remove(job)
        done.add(job)
        script.append(job)
        now += cost[job[0]]

    amplitudes = crossed = 0
    while events or jobs:
        if events and (events[0][0] <= now or not jobs):
            at, _, what = heapq.heappop(events)
            now = max(now, at)
            if what[0] == "arrive":
                _, p, stage = what
                if stage == 0 and ("rest", p) not in done:
                    run(("rest", p))
                if stage == bits - 1:
                    for job in [j for j in jobs if j[0] in ("gram", "invert")]:
                        run(job)
                    now += AMPLITUDE_US
                    amplitudes += 1
                script.append(what)
                now += STEP_US
                if stage < last:
                    send(p, stage + 1)
                if stage >= last - 1:
                    k = stage - (last - 1)
                    jobs += [("cross", p, k)] + [("fit", p, k, i) for i in range(fit_jobs)]
                if amplitudes == parts and ("sum",) not in done:
                    done.add(("sum",))
                    script.append(("sum",))
                    now += AMPLITUDE_US
                    post(max([now, *free.values()]) + HOP_US + 1.0, ("sum_near",))
            elif what[0] == "sum_near":
                script.append(what)
                now += STEP_US
                post(max([now, *free.values()]) + HOP_US + 1.5, ("sum_far",))
            else:
                script.append(what)
                if ("model",) in jobs:
                    jobs.remove(("model",))
                    script.insert(len(script) - 1, ("model",))
                jobs += [("hessian", i) for i in range(invert_jobs)]
            continue
        job = min(jobs, key=lambda j: rank[j[0]])
        if events and rank[job[0]] > 0 and events[0][0] < now + cost[job[0]] - SLACK_US:
            now = max(now, events[0][0])
            continue
        run(job)
        if job[0] == "cross":
            crossed += 1
            if crossed == 2 * parts:
                script.append(("cross_sum",))
    return script


def step_kernel(
    modes, tm_bits, sp_bits, parts,
    x_ref, exps_in,
    full, res_ref, new_ref,
    exps_ref, xbuf, yz_ref, basis, fit_basis, halves, tail, ssum, snear, sfar, vsum, vnear, vfar,
    rs_send, rs_recv, ag_send, ag_recv,
    sn_send, sn_recv, sf_send, sf_recv, n_send, n_recv, f_send, f_recv, x_sem, exps_sem,
):
    double = 2 * modes
    local_rows, columns = xbuf.shape
    width = columns // parts
    half = width // 2
    last = tm_bits - 1
    me, sp = lax.axis_index("tm"), lax.axis_index("space")
    swap = sp % 2

    def stride_of(bit):
        if tm_bits > 2 and bit == 0:
            return 1 + swap
        if tm_bits > 2 and bit == 1:
            return 2 - swap
        return 2**bit

    def flip(index, stride):
        side = (index // stride) % 2
        return side, index + (1 - 2 * side) * stride

    spaces, low = 2**sp_bits, 2 ** (tm_bits // 2)
    n_near, n_far = low * spaces, 2**tm_bits // low
    near_slot, far_slot = (me % low) * spaces + sp, me // low
    near, far = [], []
    for d in range(1, n_near):
        other = (near_slot + d) % n_near
        near.append((far_slot * low + other // spaces, other % spaces))
    for d in range(1, n_far):
        far.append(((far_slot + d) % n_far * low + me % low, sp))
    n_all = 2**tm_bits * spaces
    every, every_slot = [], me * spaces + sp
    for bits in range(n_all - 1, 0, -1):
        other = every_slot
        for b in range(tm_bits + sp_bits):
            if bits >> b & 1:
                other = flip(other, 2**b)[1]
        every.append((other // spaces, other % spaces))
    one_step = len(every) < ONE_STEP_DEVICES
    friends = every if one_step else near + far

    def lanes(start, size):
        return pl.ds(pl.multiple_of(start, LANES), size)

    orders = []
    for p in range(parts):
        order = [b for b in ORDERS[p % len(ORDERS)] if b < tm_bits]
        orders.append([b for b in range(tm_bits) if b not in order] + order)
    plan = [[flip(me, stride_of(b)) for b in order] for order in orders]

    def part_half(p, k):
        side = plan[p][0][0]
        return p * width + ((1 - side) * half if k == 0 else side * half)

    exps_load = pltpu.make_async_copy(exps_in, exps_ref, exps_sem)
    exps_load.start()
    loads = {}

    def load(p, k):
        at = lanes(part_half(p, k), half)
        loads[p, k] = pltpu.make_async_copy(x_ref.at[:, at], xbuf.at[:, at], x_sem.at[p, k])
        loads[p, k].start()

    load(0, 0)
    barrier = pltpu.get_barrier_semaphore()
    for friend in friends:
        pl.semaphore_signal(barrier, inc=1, device_id=friend, device_id_type=MESH)
    for p in range(1, parts):
        load(p, 0)

    exps_load.wait()
    rate, frequency = column_of(exps_ref[pl.ds(0, 1), :]), column_of(exps_ref[pl.ds(1, 1), :])
    total_rows = local_rows * 2**tm_bits
    steps = lax.broadcasted_iota(jnp.int32, (1, local_rows), 1)
    time = (me * local_rows + steps).astype(jnp.float32) / total_rows
    real, imag = waves(rate, frequency, time)
    plain = jnp.concatenate([real, -imag], 0)
    basis[...] = jnp.concatenate([plain, time * plain], 0).astype(jnp.bfloat16)
    for p in range(parts):
        load(p, 1)

    def project(p, k):
        loads[p, k].wait()
        at = part_half(p, k)
        tile = min(TILE, half)

        def step(i, carry):
            here = lanes(at + i * tile, tile)
            yz_ref[:, here] = jnp.dot(
                basis[...], xbuf[:, here], preferred_element_type=jnp.float32
            )
            return carry

        lax.fori_loop(0, half // tile, step, 0)

    sends = []

    def remote(src, dst, send, recv, friend):
        copy = pltpu.make_async_remote_copy(
            src_ref=src, dst_ref=dst, send_sem=send, recv_sem=recv,
            device_id=friend, device_id_type=MESH,
        )
        copy.start()
        sends.append(copy)
        return copy

    flying = {}
    above = pl.ds(0, double)

    def scatter_start(p, s):
        side, partner = plan[p][s]
        size = width >> (s + 1)
        away = (1 - side) * size
        if s == last:
            src, dst = halves[s - 1].at[p], tail.at[p]
        elif s == 0:
            src, dst = yz_ref.at[above, lanes(p * width + away, size)], halves[s].at[p]
        else:
            src, dst = halves[s - 1].at[p, :, lanes(away, size)], halves[s].at[p]
        flying[p] = remote(src, dst, rs_send.at[p, s], rs_recv.at[p, s], (partner, sp))

    def scatter_add(p, s):
        side, _ = plan[p][s]
        size = width >> (s + 1)
        if s == 0:
            mine = yz_ref[above, lanes(p * width + side * size, size)]
        else:
            mine = halves[s - 1][p, :, lanes(side * size, size)]
        halves[s][p] = halves[s][p] + mine

    offsets = []
    for p in range(parts):
        start = p * width
        for s in range(last):
            start = start + plan[p][s][0] * (width >> (s + 1))
        offsets.append(start)

    def gather_start(p, s):
        where = full.at[:, lanes(offsets[p], width >> (s + 1))]
        flying[p] = remote(
            where, where, ag_send.at[p, s], ag_recv.at[p, s], (plan[p][s][1], sp)
        )

    def gather_sum_start(source, landed, slot, peers, send, recv):
        copies = [
            remote(source, landed.at[slot], send.at[d], recv.at[d], peer)
            for d, peer in enumerate(peers)
        ]
        landed[slot] = source[...]
        return copies

    def gather_sum_end(copies, landed):
        for copy in copies:
            copy.wait_recv()
        total = landed[0]
        for k in range(1, len(copies) + 1):
            total = total + landed[k]
        return total

    for p in range(parts):
        project(p, 0)
        if p == 0:
            pl.semaphore_wait(barrier, len(friends))
        scatter_start(p, 0)

    state = {
        "self": jnp.zeros((double, double), jnp.float32),
        "cross": (jnp.zeros((modes, LANES), jnp.float32),) * 2,
    }
    square = (modes, modes)

    def gram():
        fit_basis[...] = jnp.transpose(plain).astype(jnp.bfloat16)
        base_time = steps.astype(jnp.float32) / total_rows
        base = moments(*waves(rate, frequency, base_time), base_time)
        groups = 2**tm_bits
        wide = max(LANES, groups)
        block = lax.broadcasted_iota(jnp.int32, (1, wide), 1)
        shift_time = (block * local_rows).astype(jnp.float32) / total_rows
        used = block < groups
        shift_time = jnp.where(used, shift_time, 0.0)
        turn_r, turn_i = waves(rate, frequency, shift_time)
        turn = moments(
            jnp.where(used, turn_r, 0.0), jnp.where(used, turn_i, 0.0), shift_time
        )

        def times(m, n):
            return complex_product(*turn[m], *base[n])

        g = times(0, 0)
        c = [a + b for a, b in zip(times(1, 0), times(0, 1))]
        e = [
            a + 2.0 * b + d for a, b, d in zip(times(2, 0), times(1, 1), times(0, 2))
        ]
        state.update(c=c, e=e, inverse=g)

    def finish_inverse():
        inv_r, inv_i = state["inverse"]
        state["solve"] = jnp.concatenate(
            [jnp.concatenate([inv_r, -inv_i], 1), jnp.concatenate([inv_i, inv_r], 1)], 0
        )

    def model():
        c_r, c_i = state["c"]
        t_r, t_i = complex_dot(*state["inverse"], c_r, c_i)
        u_r, u_i = complex_dot(c_r, c_i, t_r, t_i)
        state["m"] = (state["e"][0] - u_r, state["e"][1] - u_i)

    def arrive(p, stage):
        if stage < last:
            flying[p].wait_recv()
            scatter_add(p, stage)
            scatter_start(p, stage + 1)
        elif stage == last:
            flying[p].wait_recv()
            amps = exact_dot(state["solve"], halves[last - 1][p] + tail[p])
            full[:, lanes(offsets[p], width >> last)] = amps
            gather_start(p, last - 1)
            state["self"] = state["self"] + exact_dot(amps, amps, OVER_LANES)
        else:
            s = 2 * last - stage
            flying[p].wait_recv()
            offsets[p] = offsets[p] - plan[p][s][0] * (width >> (s + 1))
            if s > 0:
                gather_start(p, s - 1)

    def sum_start():
        both = state["self"]
        moved = pltpu.roll(jnp.concatenate([both, both], 1), LANES - modes, 1)
        s_r = both[:modes, :modes] + moved[modes:, :modes]
        s_i = moved[:modes, :modes] - both[modes:, :modes]
        pair = 0.5 * jnp.concatenate([s_r, s_i], 1)
        ssum[0] = jnp.concatenate([pair[: modes // 2], pair[modes // 2 :]], 1)
        state["copies"] = gather_sum_start(ssum.at[0], snear, near_slot, near, sn_send, sn_recv)

    def sum_near():
        ssum[1] = gather_sum_end(state["copies"], snear)
        state["copies"] = gather_sum_start(ssum.at[1], sfar, far_slot, far, sf_send, sf_recv)

    def sum_far():
        packed = gather_sum_end(state["copies"], sfar)

        def piece(n):
            moved = packed if n == 0 else pltpu.roll(packed, LANES - n * modes, 1)
            return moved[:, :modes]

        s_r = jnp.concatenate([piece(0), piece(2)], 0)
        s_i = jnp.concatenate([piece(1), piece(3)], 0)
        diagonal = lax.broadcasted_iota(jnp.int32, square, 0) == lax.broadcasted_iota(
            jnp.int32, square, 1
        )
        h_r, h_i = complex_product(s_r, s_i, *state["m"])
        c_r, c_i = state["c"]
        state["hessian"] = (h_r + jnp.where(diagonal, damping, 0.0), h_i)
        state["w"] = (
            jnp.sum(c_r * s_r - c_i * s_i, 1, keepdims=True),
            jnp.sum(c_r * s_i + c_i * s_r, 1, keepdims=True),
        )

    def fit_start(p, k):
        return part_half(p, 1 - k)

    def cross(p, k):
        start = fit_start(p, k)
        run = min(4, half // LANES)

        def step(i, carry):
            v_r, v_i = carry
            for j in range(run):
                at = lanes(start + (i * run + j) * LANES, LANES)
                a_r, a_i = full[pl.ds(0, modes), at], full[pl.ds(modes, modes), at]
                z_r = yz_ref[pl.ds(double, modes), at]
                z_i = yz_ref[pl.ds(double + modes, modes), at]
                v_r = v_r + (a_r * z_r + a_i * z_i)
                v_i = v_i + (a_r * z_i - a_i * z_r)
            return v_r, v_i

        state["cross"] = lax.fori_loop(0, half // (run * LANES), step, state["cross"])

    fit_jobs = max(half // FIT_TILE, 1)
    fit_tile = half // fit_jobs

    def fit(p, k, i):
        at = lanes(fit_start(p, k) + i * fit_tile, fit_tile)
        fitted = jnp.dot(
            fit_basis[...], full[:, at].astype(jnp.bfloat16), preferred_element_type=jnp.float32
        )
        res_ref[:, at] = (xbuf[:, at].astype(jnp.float32) - fitted).astype(res_ref.dtype)

    def cross_sum():
        ones = jnp.ones((8, LANES), jnp.float32)
        vsum[0] = jnp.zeros(vsum.shape[1:], jnp.float32)
        vsum[0, :, pl.ds(0, double)] = exact_dot(
            ones, jnp.concatenate(state["cross"], 0), OVER_LANES
        )
        slot, peers = (every_slot, every) if one_step else (near_slot, near)
        state["v"] = gather_sum_start(vsum.at[0], vnear, slot, peers, n_send, n_recv)

    def cross_near():
        if not one_step:
            vsum[1] = gather_sum_end(state["v"], vnear)
            state["v"] = gather_sum_start(vsum.at[1], vfar, far_slot, far, f_send, f_recv)

    invert_jobs = modes // INVERT_STEPS
    script = timeline(orders, tm_bits, width, double, invert_jobs, fit_jobs)
    at_sum = script.index(("cross_sum",))
    trailing = [i for i, job in enumerate(script) if i > at_sum and job[0] in ("fit", "hessian")]
    middle = trailing[len(trailing) // 2] if trailing else None
    passed = False
    for i, (name, *where) in enumerate(script):
        if i == middle:
            cross_near()
            passed = True
        if name == "arrive":
            arrive(*where)
        elif name == "rest":
            project(where[0], 1)
        elif name == "gram":
            gram()
        elif name == "invert":
            state["inverse"] = invert_steps(
                *state["inverse"], where[0] * INVERT_STEPS, INVERT_STEPS
            )
            if where[0] == invert_jobs - 1:
                finish_inverse()
        elif name == "hessian":
            state["hessian"] = invert_steps(
                *state["hessian"], where[0] * INVERT_STEPS, INVERT_STEPS
            )
        elif name == "model":
            model()
        elif name == "sum":
            sum_start()
        elif name == "sum_near":
            sum_near()
        elif name == "sum_far":
            sum_far()
        elif name == "cross":
            cross(*where)
        elif name == "fit":
            fit(*where)
        elif name == "cross_sum":
            cross_sum()
    if not passed:
        cross_near()
    for copy in sends:
        copy.wait_send()
    v_all = gather_sum_end(state["v"], vnear if one_step else vfar)[:1]

    wide = (modes, LANES)
    spread = lax.broadcasted_iota(jnp.int32, wide, 1) - lax.broadcasted_iota(jnp.int32, wide, 0)

    def as_column(shift):
        return jnp.sum(jnp.where(spread == shift, v_all, 0.0), 1, keepdims=True)

    grad_r = state["w"][0] - as_column(0)
    grad_i = state["w"][1] - as_column(modes)
    hinv_r, hinv_i = state["hessian"]
    new_ref[pl.ds(0, 1), :] = exps_ref[pl.ds(0, 1), :] - jnp.sum(
        hinv_r * grad_r + hinv_i * grad_i, 0, keepdims=True
    )
    new_ref[pl.ds(1, 1), :] = exps_ref[pl.ds(1, 1), :] - jnp.sum(
        hinv_r * grad_i - hinv_i * grad_r, 0, keepdims=True
    )


def step(snapshots, exponents, groups, spaces):
    modes = exponents.shape[1]
    double = 2 * modes
    local_rows, columns = snapshots.shape
    tm_bits, sp_bits = groups.bit_length() - 1, spaces.bit_length() - 1
    assert groups == 2**tm_bits and spaces == 2**sp_bits and tm_bits >= 2
    assert 4 * modes == LANES
    parts = min(len(ORDERS), columns // (groups // 2 * LANES))
    width = columns // parts
    low = 2 ** (tm_bits // 2)
    near, far = low * spaces, groups // low
    every = groups * spaces
    v_near = every if every <= ONE_STEP_DEVICES else near

    def buffer(*shape):
        return pltpu.VMEM(shape, jnp.float32)

    def dma(*shape):
        return pltpu.SemaphoreType.DMA(shape)

    vmem = pl.BlockSpec(memory_space=pltpu.VMEM)
    return pl.pallas_call(
        functools.partial(step_kernel, modes, tm_bits, sp_bits, parts),
        out_shape=(
            jax.ShapeDtypeStruct((double, columns), jnp.float32),
            jax.ShapeDtypeStruct(snapshots.shape, snapshots.dtype),
            jax.ShapeDtypeStruct(exponents.shape, jnp.float32),
        ),
        in_specs=[pl.BlockSpec(memory_space=pltpu.HBM)] * 2,
        out_specs=(vmem, vmem, vmem),
        scratch_shapes=[
            buffer(*exponents.shape),
            pltpu.VMEM((local_rows, columns), snapshots.dtype),
            buffer(2 * double, columns),
            pltpu.VMEM((2 * double, local_rows), jnp.bfloat16),
            pltpu.VMEM((local_rows, double), jnp.bfloat16),
            [buffer(parts, double, width >> (s + 1)) for s in range(tm_bits - 1)],
            buffer(parts, double, width >> (tm_bits - 1)),
            buffer(2, modes // 2, LANES),
            buffer(near, modes // 2, LANES),
            buffer(far, modes // 2, LANES),
            buffer(2, 8, LANES),
            buffer(v_near, 8, LANES),
            buffer(far, 8, LANES),
            dma(parts, tm_bits), dma(parts, tm_bits),
            dma(parts, tm_bits), dma(parts, tm_bits),
            dma(near - 1), dma(near - 1),
            dma(far - 1), dma(far - 1),
            dma(v_near - 1), dma(v_near - 1),
            dma(far - 1), dma(far - 1),
            dma(parts, 2),
            pltpu.SemaphoreType.DMA,
        ],
        compiler_params=pltpu.CompilerParams(
            collective_id=0, has_side_effects=True, vmem_limit_bytes=40 * 2**20
        ),
    )(snapshots, exponents)


def write_kernel(pieces, *refs):
    sources, targets, sem = refs[:3], refs[3:6], refs[6]
    copies = []
    for i, (source, target) in enumerate(zip(sources, targets)):
        rows = source.shape[0] // pieces[i]
        for j in range(pieces[i]):
            part = pl.ds(j * rows, rows)
            copies.append((source.at[part], target.at[part]))
    copies = [
        pltpu.make_async_copy(source, target, sem.at[i])
        for i, (source, target) in enumerate(copies)
    ]
    for copy in copies:
        copy.start()
    for copy in copies:
        copy.wait()


def write(residual, amp_rows, new_exponents):
    pieces = (8, 2, 1)
    arrays = (residual, amp_rows, new_exponents)
    return pl.pallas_call(
        functools.partial(write_kernel, pieces),
        out_shape=tuple(jax.ShapeDtypeStruct(a.shape, a.dtype) for a in arrays),
        in_specs=[pl.BlockSpec(memory_space=pltpu.VMEM)] * 3,
        out_specs=[pl.BlockSpec(memory_space=pltpu.HBM)] * 3,
        scratch_shapes=[pltpu.SemaphoreType.DMA((sum(pieces),))],
        compiler_params=pltpu.CompilerParams(vmem_limit_bytes=24 * 2**20),
    )(*arrays)


def shards(snapshots, exponents):
    columns = snapshots.shape[1]
    modes = exponents.shape[1]
    groups, spaces = lax.axis_size("tm"), lax.axis_size("space")
    amp_rows, residual, new_exponents = step(snapshots, exponents, groups, spaces)
    residual, amp_rows, new_exponents = write(residual, amp_rows, new_exponents)
    return (new_exponents, amp_rows.reshape(2, modes, columns), residual)


def solution(mesh):
    return jax.shard_map(
        shards,
        mesh=mesh,
        in_specs=(P("tm", "space"), P()),
        out_specs=(P(), P(None, None, "space"), P("tm", "space")),
        check_vma=False,
    )
```

```python
import functools
import heapq

import jax
import jax.numpy as jnp
from jax import lax
from jax.experimental import pallas as pl
from jax.experimental.pallas import tpu as pltpu
from jax.sharding import PartitionSpec as P

damping = 0.01
MESH = pl.DeviceIdType.MESH
LANES = 128
TILE = 512
FIT_TILE = 256
INVERT_STEPS = 2
ORDERS = (
    (3, 0, 2, 1), (0, 2, 1, 3), (0, 1, 2, 3), (1, 0, 3, 2), (0, 1, 3, 2), (2, 0, 1, 3), (2, 0, 1, 3), (0, 1, 2, 3),
)
ONE_STEP_DEVICES = 32
OVER_LANES = ((1,), (1,))

LINK_BYTES_PER_US = 100e3
HOP_US = 2.45
FAR_US = 0.42
STEP_US = 0.4
PROJECT_US = 0.25
AMPLITUDE_US = 0.45
GRAM_US = 1.0
INVERT_US = 0.18
MODEL_US = 0.6
CROSS_US = 0.05
FIT_US = 0.23
SLACK_US = 0.1
START_US = 1.7


def exact_dot(left, right, dims=((1,), (0,))):
    return lax.dot_general(
        left,
        right,
        (dims, ((), ())),
        precision=lax.Precision.HIGHEST,
        preferred_element_type=jnp.float32,
    )


def complex_dot(ar, ai, br, bi):
    return exact_dot(ar, br) - exact_dot(ai, bi), exact_dot(ar, bi) + exact_dot(ai, br)


def complex_product(ar, ai, br, bi):
    return ar * br - ai * bi, ar * bi + ai * br


def invert_steps(real, imag, first, count):
    rows = lax.broadcasted_iota(jnp.int32, real.shape, 0)
    cols = lax.broadcasted_iota(jnp.int32, real.shape, 1)
    for k in range(first, first + count):
        on_row, on_col = rows == k, cols == k
        scale = 1.0 / real[k : k + 1, k : k + 1]
        row_r = jnp.where(on_col[:1], 1.0, real[k : k + 1, :]) * scale
        row_i = jnp.where(on_col[:1], 0.0, imag[k : k + 1, :]) * scale
        col_r, col_i = real[:, k : k + 1], imag[:, k : k + 1]
        real = jnp.where(
            on_row, row_r, jnp.where(on_col, 0.0, real) - (col_r * row_r - col_i * row_i)
        )
        imag = jnp.where(
            on_row, row_i, jnp.where(on_col, 0.0, imag) - (col_r * row_i + col_i * row_r)
        )
    return real, imag


def column_of(row):
    n = row.shape[1]
    here = lax.broadcasted_iota(jnp.int32, (n, n), 0) == lax.broadcasted_iota(
        jnp.int32, (n, n), 1
    )
    return jnp.sum(jnp.where(here, row, 0.0), 1, keepdims=True)


def waves(rate, frequency, time):
    magnitude = jnp.exp(time * rate)
    angle = time * frequency
    return magnitude * jnp.cos(angle), magnitude * jnp.sin(angle)


def moments(real, imag, time):
    modes = real.shape[0]
    both = jnp.concatenate(
        [jnp.concatenate([real, imag], 1), jnp.concatenate([-imag, real], 1)], 0
    )
    first, twice = both[:modes], jnp.concatenate([time, time], 1)
    powers = [first, twice * first, twice * (twice * first)]
    powers += [jnp.zeros_like(first)] * (LANES // modes - len(powers))
    sums = exact_dot(both, jnp.concatenate(powers, 0), OVER_LANES)
    blocks = []
    for n in range(3):
        moved = sums if n == 0 else pltpu.roll(sums, LANES - n * modes, 1)
        blocks.append((moved[:modes, :modes], moved[modes:, :modes]))
    return blocks


def timeline(orders, bits, width, rows, invert_jobs, fit_jobs):
    parts, last = len(orders), 2 * bits - 2
    free = {}
    events, script, count = [], [], [0]
    done = set()
    now = START_US

    def post(at, what):
        heapq.heappush(events, (at, count[0], what))
        count[0] += 1

    def send(p, stage):
        s = min(stage, last - stage)
        bit = orders[p][s]
        size = (width >> min(s + 1, bits - 1)) * rows * 4 / LINK_BYTES_PER_US
        delay = HOP_US
        if bit < 2:
            keys = {"xy": size}
        elif bit == 2:
            keys = {"near": 2 * size}
        else:
            keys, delay = {"near": 2 * size, "far": 4 * size}, HOP_US + FAR_US
        start = max([now] + [free.get(k, 0.0) for k in keys])
        for k, v in keys.items():
            free[k] = start + v
        post(start + max(keys.values()) + delay, ("arrive", p, stage))

    for p in range(parts):
        now += PROJECT_US
        send(p, 0)
    jobs = [("rest", p) for p in range(parts)] + [("gram",)]
    jobs += [("invert", i) for i in range(invert_jobs)] + [("model",)]
    cost = {
        "rest": PROJECT_US, "gram": GRAM_US, "invert": INVERT_US, "model": MODEL_US,
        "hessian": INVERT_US, "cross": CROSS_US, "fit": FIT_US,
    }
    rank = {
        "rest": 0, "gram": 1, "invert": 2, "cross": 3, "hessian": 4, "model": 5, "fit": 6,
    }

    def run(job):
        nonlocal now
        jobs.remove(job)
        done.add(job)
        script.append(job)
        now += cost[job[0]]

    amplitudes = crossed = 0
    while events or jobs:
        if events and (events[0][0] <= now or not jobs):
            at, _, what = heapq.heappop(events)
            now = max(now, at)
            if what[0] == "arrive":
                _, p, stage = what
                if stage == 0 and ("rest", p) not in done:
                    run(("rest", p))
                if stage == bits - 1:
                    for job in [j for j in jobs if j[0] in ("gram", "invert")]:
                        run(job)
                    now += AMPLITUDE_US
                    amplitudes += 1
                script.append(what)
                now += STEP_US
                if stage < last:
                    send(p, stage + 1)
                if stage >= last - 1:
                    k = stage - (last - 1)
                    jobs += [("cross", p, k)] + [("fit", p, k, i) for i in range(fit_jobs)]
                if amplitudes == parts and ("sum",) not in done:
                    done.add(("sum",))
                    script.append(("sum",))
                    now += AMPLITUDE_US
                    post(max([now, *free.values()]) + HOP_US + 1.0, ("sum_near",))
            elif what[0] == "sum_near":
                script.append(what)
                now += STEP_US
                post(max([now, *free.values()]) + HOP_US + 1.5, ("sum_far",))
            else:
                script.append(what)
                if ("model",) in jobs:
                    jobs.remove(("model",))
                    script.insert(len(script) - 1, ("model",))
                jobs += [("hessian", i) for i in range(invert_jobs)]
            continue
        job = min(jobs, key=lambda j: rank[j[0]])
        if events and rank[job[0]] > 0 and events[0][0] < now + cost[job[0]] - SLACK_US:
            now = max(now, events[0][0])
            continue
        run(job)
        if job[0] == "cross":
            crossed += 1
            if crossed == 2 * parts:
                script.append(("cross_sum",))
    at, known = script.index(("cross_sum",)), script.index(("sum_far",))
    if known > at:
        script.insert(known, script.pop(at))
    return script


def step_kernel(
    modes, tm_bits, sp_bits, parts,
    x_ref, exps_in,
    full, res_ref, new_ref,
    exps_ref, xbuf, yz_ref, basis, fit_basis, halves, tail, ssum, snear, sfar, vsum, vnear, vfar,
    rs_send, rs_recv, ag_send, ag_recv,
    sn_send, sn_recv, sf_send, sf_recv, n_send, n_recv, f_send, f_recv, x_sem, exps_sem,
):
    double = 2 * modes
    local_rows, columns = xbuf.shape
    width = columns // parts
    half = width // 2
    last = tm_bits - 1
    me, sp = lax.axis_index("tm"), lax.axis_index("space")
    swap = sp % 2

    def stride_of(bit):
        if tm_bits > 2 and bit == 0:
            return 1 + swap
        if tm_bits > 2 and bit == 1:
            return 2 - swap
        return 2**bit

    def flip(index, stride):
        side = (index // stride) % 2
        return side, index + (1 - 2 * side) * stride

    spaces, low = 2**sp_bits, 2 ** (tm_bits // 2)
    n_near, n_far = low * spaces, 2**tm_bits // low
    near_slot, far_slot = (me % low) * spaces + sp, me // low
    near, far = [], []
    for d in range(1, n_near):
        other = (near_slot + d) % n_near
        near.append((far_slot * low + other // spaces, other % spaces))
    for d in range(1, n_far):
        far.append(((far_slot + d) % n_far * low + me % low, sp))
    n_all = 2**tm_bits * spaces
    every, every_slot = [], me * spaces + sp
    for bits in range(n_all - 1, 0, -1):
        other = every_slot
        for b in range(tm_bits + sp_bits):
            if bits >> b & 1:
                other = flip(other, 2**b)[1]
        every.append((other // spaces, other % spaces))
    one_step = len(every) < ONE_STEP_DEVICES
    friends = near + far

    def lanes(start, size):
        return pl.ds(pl.multiple_of(start, LANES), size)

    orders = []
    for p in range(parts):
        order = [b for b in ORDERS[p % len(ORDERS)] if b < tm_bits]
        orders.append([b for b in range(tm_bits) if b not in order] + order)
    plan = [[flip(me, stride_of(b)) for b in order] for order in orders]

    def part_half(p, k):
        side = plan[p][0][0]
        return p * width + ((1 - side) * half if k == 0 else side * half)

    exps_load = pltpu.make_async_copy(exps_in, exps_ref, exps_sem)
    exps_load.start()
    loads = {}

    def load(p, k):
        at = lanes(part_half(p, k), half)
        loads[p, k] = pltpu.make_async_copy(x_ref.at[:, at], xbuf.at[:, at], x_sem.at[p, k])
        loads[p, k].start()

    load(0, 0)
    barrier = pltpu.get_barrier_semaphore()
    for friend in friends:
        pl.semaphore_signal(barrier, inc=1, device_id=friend, device_id_type=MESH)
    for p in range(1, parts):
        load(p, 0)

    exps_load.wait()
    rate, frequency = column_of(exps_ref[pl.ds(0, 1), :]), column_of(exps_ref[pl.ds(1, 1), :])
    total_rows = local_rows * 2**tm_bits
    steps = lax.broadcasted_iota(jnp.int32, (1, local_rows), 1)
    time = (me * local_rows + steps).astype(jnp.float32) / total_rows
    real, imag = waves(rate, frequency, time)
    plain = jnp.concatenate([real, -imag], 0)
    basis[...] = jnp.concatenate([plain, time * plain], 0).astype(jnp.bfloat16)
    for p in range(parts):
        load(p, 1)

    def project(p, k):
        loads[p, k].wait()
        at = part_half(p, k)
        tile = min(TILE, half)

        def step(i, carry):
            here = lanes(at + i * tile, tile)
            yz_ref[:, here] = jnp.dot(
                basis[...], xbuf[:, here], preferred_element_type=jnp.float32
            )
            return carry

        lax.fori_loop(0, half // tile, step, 0)

    sends = []

    def remote(src, dst, send, recv, friend):
        copy = pltpu.make_async_remote_copy(
            src_ref=src, dst_ref=dst, send_sem=send, recv_sem=recv,
            device_id=friend, device_id_type=MESH,
        )
        copy.start()
        sends.append(copy)
        return copy

    flying = {}
    above = pl.ds(0, double)

    def scatter_start(p, s):
        side, partner = plan[p][s]
        size = width >> (s + 1)
        away = (1 - side) * size
        if s == last:
            src, dst = halves[s - 1].at[p], tail.at[p]
        elif s == 0:
            src, dst = yz_ref.at[above, lanes(p * width + away, size)], halves[s].at[p]
        else:
            src, dst = halves[s - 1].at[p, :, lanes(away, size)], halves[s].at[p]
        flying[p] = remote(src, dst, rs_send.at[p, s], rs_recv.at[p, s], (partner, sp))

    def scatter_add(p, s):
        side, _ = plan[p][s]
        size = width >> (s + 1)
        if s == 0:
            mine = yz_ref[above, lanes(p * width + side * size, size)]
        else:
            mine = halves[s - 1][p, :, lanes(side * size, size)]
        halves[s][p] = halves[s][p] + mine

    offsets = []
    for p in range(parts):
        start = p * width
        for s in range(last):
            start = start + plan[p][s][0] * (width >> (s + 1))
        offsets.append(start)

    def gather_start(p, s):
        where = full.at[:, lanes(offsets[p], width >> (s + 1))]
        flying[p] = remote(
            where, where, ag_send.at[p, s], ag_recv.at[p, s], (plan[p][s][1], sp)
        )

    def gather_sum_start(source, landed, slot, peers, send, recv):
        copies = [
            remote(source, landed.at[slot], send.at[d], recv.at[d], peer)
            for d, peer in enumerate(peers)
        ]
        landed[slot] = source[...]
        return copies

    def gather_sum_end(copies, landed):
        for copy in copies:
            copy.wait_recv()
        total = landed[0]
        for k in range(1, len(copies) + 1):
            total = total + landed[k]
        return total

    for p in range(parts):
        project(p, 0)
        if p == 0:
            pl.semaphore_wait(barrier, len(friends))
        scatter_start(p, 0)

    state = {
        "self": jnp.zeros((double, double), jnp.float32),
        "cross": (jnp.zeros((modes, LANES), jnp.float32),) * 2,
    }
    square = (modes, modes)

    def gram():
        fit_basis[...] = jnp.transpose(plain).astype(jnp.bfloat16)
        base_time = steps.astype(jnp.float32) / total_rows
        base = moments(*waves(rate, frequency, base_time), base_time)
        groups = 2**tm_bits
        wide = max(LANES, groups)
        block = lax.broadcasted_iota(jnp.int32, (1, wide), 1)
        shift_time = (block * local_rows).astype(jnp.float32) / total_rows
        used = block < groups
        shift_time = jnp.where(used, shift_time, 0.0)
        turn_r, turn_i = waves(rate, frequency, shift_time)
        turn = moments(
            jnp.where(used, turn_r, 0.0), jnp.where(used, turn_i, 0.0), shift_time
        )

        def times(m, n):
            return complex_product(*turn[m], *base[n])

        g = times(0, 0)
        c = [a + b for a, b in zip(times(1, 0), times(0, 1))]
        e = [
            a + 2.0 * b + d for a, b, d in zip(times(2, 0), times(1, 1), times(0, 2))
        ]
        state.update(c=c, e=e, inverse=g)

    def finish_inverse():
        inv_r, inv_i = state["inverse"]
        state["solve"] = jnp.concatenate(
            [jnp.concatenate([inv_r, -inv_i], 1), jnp.concatenate([inv_i, inv_r], 1)], 0
        )

    def model():
        c_r, c_i = state["c"]
        t_r, t_i = complex_dot(*state["inverse"], c_r, c_i)
        u_r, u_i = complex_dot(c_r, c_i, t_r, t_i)
        state["m"] = (state["e"][0] - u_r, state["e"][1] - u_i)

    def arrive(p, stage):
        if stage < last:
            flying[p].wait_recv()
            scatter_add(p, stage)
            scatter_start(p, stage + 1)
        elif stage == last:
            flying[p].wait_recv()
            amps = exact_dot(state["solve"], halves[last - 1][p] + tail[p])
            full[:, lanes(offsets[p], width >> last)] = amps
            gather_start(p, last - 1)
            state["self"] = state["self"] + exact_dot(amps, amps, OVER_LANES)
        else:
            s = 2 * last - stage
            flying[p].wait_recv()
            offsets[p] = offsets[p] - plan[p][s][0] * (width >> (s + 1))
            if s > 0:
                gather_start(p, s - 1)

    def sum_start():
        both = state["self"]
        moved = pltpu.roll(jnp.concatenate([both, both], 1), LANES - modes, 1)
        s_r = both[:modes, :modes] + moved[modes:, :modes]
        s_i = moved[:modes, :modes] - both[modes:, :modes]
        pair = 0.5 * jnp.concatenate([s_r, s_i], 1)
        ssum[0] = jnp.concatenate([pair[: modes // 2], pair[modes // 2 :]], 1)
        state["copies"] = gather_sum_start(ssum.at[0], snear, near_slot, near, sn_send, sn_recv)

    def sum_near():
        ssum[1] = gather_sum_end(state["copies"], snear)
        state["copies"] = gather_sum_start(ssum.at[1], sfar, far_slot, far, sf_send, sf_recv)

    def sum_far():
        packed = gather_sum_end(state["copies"], sfar)

        def piece(n):
            moved = packed if n == 0 else pltpu.roll(packed, LANES - n * modes, 1)
            return moved[:, :modes]

        s_r = jnp.concatenate([piece(0), piece(2)], 0)
        s_i = jnp.concatenate([piece(1), piece(3)], 0)
        diagonal = lax.broadcasted_iota(jnp.int32, square, 0) == lax.broadcasted_iota(
            jnp.int32, square, 1
        )
        h_r, h_i = complex_product(s_r, s_i, *state["m"])
        c_r, c_i = state["c"]
        state["hessian"] = (h_r + jnp.where(diagonal, damping, 0.0), h_i)
        state["w"] = (
            jnp.sum(c_r * s_r - c_i * s_i, 1, keepdims=True),
            jnp.sum(c_r * s_i + c_i * s_r, 1, keepdims=True),
        )

    def fit_start(p, k):
        return part_half(p, 1 - k)

    def cross(p, k):
        start = fit_start(p, k)
        run = min(4, half // LANES)

        def step(i, carry):
            v_r, v_i = carry
            for j in range(run):
                at = lanes(start + (i * run + j) * LANES, LANES)
                a_r, a_i = full[pl.ds(0, modes), at], full[pl.ds(modes, modes), at]
                z_r = yz_ref[pl.ds(double, modes), at]
                z_i = yz_ref[pl.ds(double + modes, modes), at]
                v_r = v_r + (a_r * z_r + a_i * z_i)
                v_i = v_i + (a_r * z_i - a_i * z_r)
            return v_r, v_i

        state["cross"] = lax.fori_loop(0, half // (run * LANES), step, state["cross"])

    fit_jobs = max(half // FIT_TILE, 1)
    fit_tile = half // fit_jobs

    def fit(p, k, i):
        at = lanes(fit_start(p, k) + i * fit_tile, fit_tile)
        fitted = jnp.dot(
            fit_basis[...], full[:, at].astype(jnp.bfloat16), preferred_element_type=jnp.float32
        )
        res_ref[:, at] = (xbuf[:, at].astype(jnp.float32) - fitted).astype(res_ref.dtype)

    def cross_sum():
        ones = jnp.ones((8, LANES), jnp.float32)
        vsum[0] = jnp.zeros(vsum.shape[1:], jnp.float32)
        vsum[0, :, pl.ds(0, double)] = exact_dot(
            ones, jnp.concatenate(state["cross"], 0), OVER_LANES
        )
        slot, peers = (every_slot, every) if one_step else (near_slot, near)
        state["v"] = gather_sum_start(vsum.at[0], vnear, slot, peers, n_send, n_recv)

    def cross_near():
        if not one_step:
            vsum[1] = gather_sum_end(state["v"], vnear)
            state["v"] = gather_sum_start(vsum.at[1], vfar, far_slot, far, f_send, f_recv)

    invert_jobs = modes // INVERT_STEPS
    script = timeline(orders, tm_bits, width, double, invert_jobs, fit_jobs)
    at_sum = script.index(("cross_sum",))
    trailing = [i for i, job in enumerate(script) if i > at_sum and job[0] in ("fit", "hessian")]
    middle = trailing[len(trailing) // 2] if trailing else None
    passed = False
    for i, (name, *where) in enumerate(script):
        if i == middle:
            cross_near()
            passed = True
        if name == "arrive":
            arrive(*where)
        elif name == "rest":
            project(where[0], 1)
        elif name == "gram":
            gram()
        elif name == "invert":
            state["inverse"] = invert_steps(
                *state["inverse"], where[0] * INVERT_STEPS, INVERT_STEPS
            )
            if where[0] == invert_jobs - 1:
                finish_inverse()
        elif name == "hessian":
            state["hessian"] = invert_steps(
                *state["hessian"], where[0] * INVERT_STEPS, INVERT_STEPS
            )
        elif name == "model":
            model()
        elif name == "sum":
            sum_start()
        elif name == "sum_near":
            sum_near()
        elif name == "sum_far":
            sum_far()
        elif name == "cross":
            cross(*where)
        elif name == "fit":
            fit(*where)
        elif name == "cross_sum":
            cross_sum()
    if not passed:
        cross_near()
    for copy in sends:
        copy.wait_send()
    v_all = gather_sum_end(state["v"], vnear if one_step else vfar)[:1]

    wide = (modes, LANES)
    spread = lax.broadcasted_iota(jnp.int32, wide, 1) - lax.broadcasted_iota(jnp.int32, wide, 0)

    def as_column(shift):
        return jnp.sum(jnp.where(spread == shift, v_all, 0.0), 1, keepdims=True)

    grad_r = state["w"][0] - as_column(0)
    grad_i = state["w"][1] - as_column(modes)
    hinv_r, hinv_i = state["hessian"]
    new_ref[pl.ds(0, 1), :] = exps_ref[pl.ds(0, 1), :] - jnp.sum(
        hinv_r * grad_r + hinv_i * grad_i, 0, keepdims=True
    )
    new_ref[pl.ds(1, 1), :] = exps_ref[pl.ds(1, 1), :] - jnp.sum(
        hinv_r * grad_i - hinv_i * grad_r, 0, keepdims=True
    )


def step(snapshots, exponents, groups, spaces):
    modes = exponents.shape[1]
    double = 2 * modes
    local_rows, columns = snapshots.shape
    tm_bits, sp_bits = groups.bit_length() - 1, spaces.bit_length() - 1
    assert groups == 2**tm_bits and spaces == 2**sp_bits and tm_bits >= 2
    assert 4 * modes == LANES
    parts = min(len(ORDERS), columns // (groups // 2 * LANES))
    width = columns // parts
    low = 2 ** (tm_bits // 2)
    near, far = low * spaces, groups // low
    every = groups * spaces
    v_near = every if every <= ONE_STEP_DEVICES else near

    def buffer(*shape):
        return pltpu.VMEM(shape, jnp.float32)

    def dma(*shape):
        return pltpu.SemaphoreType.DMA(shape)

    vmem = pl.BlockSpec(memory_space=pltpu.VMEM)
    return pl.pallas_call(
        functools.partial(step_kernel, modes, tm_bits, sp_bits, parts),
        out_shape=(
            jax.ShapeDtypeStruct((double, columns), jnp.float32),
            jax.ShapeDtypeStruct(snapshots.shape, snapshots.dtype),
            jax.ShapeDtypeStruct(exponents.shape, jnp.float32),
        ),
        in_specs=[pl.BlockSpec(memory_space=pltpu.HBM)] * 2,
        out_specs=(vmem, vmem, vmem),
        scratch_shapes=[
            buffer(*exponents.shape),
            pltpu.VMEM((local_rows, columns), snapshots.dtype),
            buffer(2 * double, columns),
            pltpu.VMEM((2 * double, local_rows), jnp.bfloat16),
            pltpu.VMEM((local_rows, double), jnp.bfloat16),
            [buffer(parts, double, width >> (s + 1)) for s in range(tm_bits - 1)],
            buffer(parts, double, width >> (tm_bits - 1)),
            buffer(2, modes // 2, LANES),
            buffer(near, modes // 2, LANES),
            buffer(far, modes // 2, LANES),
            buffer(2, 8, LANES),
            buffer(v_near, 8, LANES),
            buffer(far, 8, LANES),
            dma(parts, tm_bits), dma(parts, tm_bits),
            dma(parts, tm_bits), dma(parts, tm_bits),
            dma(near - 1), dma(near - 1),
            dma(far - 1), dma(far - 1),
            dma(v_near - 1), dma(v_near - 1),
            dma(far - 1), dma(far - 1),
            dma(parts, 2),
            pltpu.SemaphoreType.DMA,
        ],
        compiler_params=pltpu.CompilerParams(
            collective_id=0, has_side_effects=True, vmem_limit_bytes=40 * 2**20
        ),
    )(snapshots, exponents)


def write_kernel(pieces, *refs):
    sources, targets, sem = refs[:3], refs[3:6], refs[6]
    copies = []
    for i, (source, target) in enumerate(zip(sources, targets)):
        rows = source.shape[0] // pieces[i]
        for j in range(pieces[i]):
            part = pl.ds(j * rows, rows)
            copies.append((source.at[part], target.at[part]))
    copies = [
        pltpu.make_async_copy(source, target, sem.at[i])
        for i, (source, target) in enumerate(copies)
    ]
    for copy in copies:
        copy.start()
    for copy in copies:
        copy.wait()


def write(residual, amp_rows, new_exponents):
    pieces = (8, 2, 1)
    arrays = (residual, amp_rows, new_exponents)
    return pl.pallas_call(
        functools.partial(write_kernel, pieces),
        out_shape=tuple(jax.ShapeDtypeStruct(a.shape, a.dtype) for a in arrays),
        in_specs=[pl.BlockSpec(memory_space=pltpu.VMEM)] * 3,
        out_specs=[pl.BlockSpec(memory_space=pltpu.HBM)] * 3,
        scratch_shapes=[pltpu.SemaphoreType.DMA((sum(pieces),))],
        compiler_params=pltpu.CompilerParams(vmem_limit_bytes=24 * 2**20),
    )(*arrays)


def shards(snapshots, exponents):
    columns = snapshots.shape[1]
    modes = exponents.shape[1]
    groups, spaces = lax.axis_size("tm"), lax.axis_size("space")
    amp_rows, residual, new_exponents = step(snapshots, exponents, groups, spaces)
    residual, amp_rows, new_exponents = write(residual, amp_rows, new_exponents)
    return (new_exponents, amp_rows.reshape(2, modes, columns), residual)


def solution(mesh):
    return jax.shard_map(
        shards,
        mesh=mesh,
        in_specs=(P("tm", "space"), P()),
        out_specs=(P(), P(None, None, "space"), P("tm", "space")),
        check_vma=False,
    )
```

```python
import functools
import heapq

import jax
import jax.numpy as jnp
from jax import lax
from jax.experimental import pallas as pl
from jax.experimental.pallas import tpu as pltpu
from jax.sharding import PartitionSpec as P

damping = 0.01
MESH = pl.DeviceIdType.MESH
LANES = 128
TILE = 512
FIT_TILE = 256
INVERT_STEPS = 2
ORDERS = (
    (3, 0, 2, 1), (0, 2, 1, 3), (0, 1, 2, 3), (1, 0, 3, 2), (0, 1, 3, 2), (2, 0, 1, 3), (2, 0, 1, 3), (0, 1, 2, 3),
)
ONE_STEP_DEVICES = 32
OVER_LANES = ((1,), (1,))

LINK_BYTES_PER_US = 94e3
HOP_US = 2.45
FAR_US = 0.42
STEP_US = 0.4
PROJECT_US = 0.25
AMPLITUDE_US = 0.45
GRAM_US = 1.0
INVERT_US = 0.18
MODEL_US = 0.6
CROSS_US = 0.05
FIT_US = 0.23
SLACK_US = 0.1
START_US = 2.3


def exact_dot(left, right, dims=((1,), (0,))):
    return lax.dot_general(
        left,
        right,
        (dims, ((), ())),
        precision=lax.Precision.HIGHEST,
        preferred_element_type=jnp.float32,
    )


def complex_dot(ar, ai, br, bi):
    return exact_dot(ar, br) - exact_dot(ai, bi), exact_dot(ar, bi) + exact_dot(ai, br)


def complex_product(ar, ai, br, bi):
    return ar * br - ai * bi, ar * bi + ai * br


def invert_steps(real, imag, first, count):
    rows = lax.broadcasted_iota(jnp.int32, real.shape, 0)
    cols = lax.broadcasted_iota(jnp.int32, real.shape, 1)
    for k in range(first, first + count):
        on_row, on_col = rows == k, cols == k
        scale = 1.0 / real[k : k + 1, k : k + 1]
        row_r = jnp.where(on_col[:1], 1.0, real[k : k + 1, :]) * scale
        row_i = jnp.where(on_col[:1], 0.0, imag[k : k + 1, :]) * scale
        col_r, col_i = real[:, k : k + 1], imag[:, k : k + 1]
        real = jnp.where(
            on_row, row_r, jnp.where(on_col, 0.0, real) - (col_r * row_r - col_i * row_i)
        )
        imag = jnp.where(
            on_row, row_i, jnp.where(on_col, 0.0, imag) - (col_r * row_i + col_i * row_r)
        )
    return real, imag


def column_of(row):
    n = row.shape[1]
    here = lax.broadcasted_iota(jnp.int32, (n, n), 0) == lax.broadcasted_iota(
        jnp.int32, (n, n), 1
    )
    return jnp.sum(jnp.where(here, row, 0.0), 1, keepdims=True)


def waves(rate, frequency, time):
    magnitude = jnp.exp(time * rate)
    angle = time * frequency
    return magnitude * jnp.cos(angle), magnitude * jnp.sin(angle)


def moments(real, imag, time):
    modes = real.shape[0]
    both = jnp.concatenate(
        [jnp.concatenate([real, imag], 1), jnp.concatenate([-imag, real], 1)], 0
    )
    first, twice = both[:modes], jnp.concatenate([time, time], 1)
    powers = [first, twice * first, twice * (twice * first)]
    powers += [jnp.zeros_like(first)] * (LANES // modes - len(powers))
    sums = exact_dot(both, jnp.concatenate(powers, 0), OVER_LANES)
    blocks = []
    for n in range(3):
        moved = sums if n == 0 else pltpu.roll(sums, LANES - n * modes, 1)
        blocks.append((moved[:modes, :modes], moved[modes:, :modes]))
    return blocks


def timeline(orders, bits, width, rows, invert_jobs, fit_jobs):
    parts, last = len(orders), 2 * bits - 2
    free = {}
    events, script, count = [], [], [0]
    done = set()
    now = START_US

    def post(at, what):
        heapq.heappush(events, (at, count[0], what))
        count[0] += 1

    def send(p, stage):
        s = min(stage, last - stage)
        bit = orders[p][s]
        size = (width >> min(s + 1, bits - 1)) * rows * 4 / LINK_BYTES_PER_US
        delay = HOP_US
        if bit < 2:
            keys = {"xy": size}
        elif bit == 2:
            keys = {"near": 2 * size}
        else:
            keys, delay = {"near": 2 * size, "far": 4 * size}, HOP_US + FAR_US
        start = max([now] + [free.get(k, 0.0) for k in keys])
        for k, v in keys.items():
            free[k] = start + v
        post(start + max(keys.values()) + delay, ("arrive", p, stage))

    for p in range(parts):
        now += PROJECT_US
        send(p, 0)
    jobs = [("rest", p) for p in range(parts)] + [("gram",)]
    jobs += [("invert", i) for i in range(invert_jobs)] + [("model",)]
    cost = {
        "rest": PROJECT_US, "gram": GRAM_US, "invert": INVERT_US, "model": MODEL_US,
        "hessian": INVERT_US, "cross": CROSS_US, "fit": FIT_US,
    }
    rank = {
        "rest": 0, "gram": 1, "invert": 2, "cross": 3, "hessian": 4, "model": 5, "fit": 6,
    }

    def run(job):
        nonlocal now
        jobs.remove(job)
        done.add(job)
        script.append(job)
        now += cost[job[0]]

    amplitudes = crossed = 0
    while events or jobs:
        if events and (events[0][0] <= now or not jobs):
            at, _, what = heapq.heappop(events)
            now = max(now, at)
            if what[0] == "arrive":
                _, p, stage = what
                if stage == 0 and ("rest", p) not in done:
                    run(("rest", p))
                if stage == bits - 1:
                    for job in [j for j in jobs if j[0] in ("gram", "invert")]:
                        run(job)
                    now += AMPLITUDE_US
                    amplitudes += 1
                script.append(what)
                now += STEP_US
                if stage < last:
                    send(p, stage + 1)
                if stage >= last - 1:
                    k = stage - (last - 1)
                    jobs += [("cross", p, k)] + [("fit", p, k, i) for i in range(fit_jobs)]
                if amplitudes == parts and ("sum",) not in done:
                    done.add(("sum",))
                    script.append(("sum",))
                    now += AMPLITUDE_US
                    post(max([now, *free.values()]) + HOP_US + 1.0, ("sum_near",))
            elif what[0] == "sum_near":
                script.append(what)
                now += STEP_US
                post(max([now, *free.values()]) + HOP_US + 1.5, ("sum_far",))
            else:
                script.append(what)
                if ("model",) in jobs:
                    jobs.remove(("model",))
                    script.insert(len(script) - 1, ("model",))
                jobs += [("hessian", i) for i in range(invert_jobs)]
            continue
        job = min(jobs, key=lambda j: rank[j[0]])
        if events and rank[job[0]] > 0 and events[0][0] < now + cost[job[0]] - SLACK_US:
            now = max(now, events[0][0])
            continue
        run(job)
        if job[0] == "cross":
            crossed += 1
            if crossed == 2 * parts:
                script.append(("cross_sum",))
    at, known = script.index(("cross_sum",)), script.index(("sum_far",))
    if known > at:
        script.insert(known, script.pop(at))
    return script


def step_kernel(
    modes, tm_bits, sp_bits, parts,
    x_ref, exps_in,
    full, res_ref, new_ref,
    exps_ref, xbuf, yz_ref, basis, fit_basis, halves, tail, ssum, snear, sfar, vsum, vnear, vfar,
    rs_send, rs_recv, ag_send, ag_recv,
    sn_send, sn_recv, sf_send, sf_recv, n_send, n_recv, f_send, f_recv, x_sem, exps_sem,
):
    double = 2 * modes
    local_rows, columns = xbuf.shape
    width = columns // parts
    half = width // 2
    last = tm_bits - 1
    me, sp = lax.axis_index("tm"), lax.axis_index("space")
    swap = sp % 2

    def stride_of(bit):
        if tm_bits > 2 and bit == 0:
            return 1 + swap
        if tm_bits > 2 and bit == 1:
            return 2 - swap
        return 2**bit

    def flip(index, stride):
        side = (index // stride) % 2
        return side, index + (1 - 2 * side) * stride

    spaces, low = 2**sp_bits, 2 ** (tm_bits // 2)
    n_near, n_far = low * spaces, 2**tm_bits // low
    near_slot, far_slot = (me % low) * spaces + sp, me // low
    near, far = [], []
    for d in range(1, n_near):
        other = (near_slot + d) % n_near
        near.append((far_slot * low + other // spaces, other % spaces))
    for d in range(1, n_far):
        far.append(((far_slot + d) % n_far * low + me % low, sp))
    n_all = 2**tm_bits * spaces
    every, every_slot = [], me * spaces + sp
    for bits in range(n_all - 1, 0, -1):
        other = every_slot
        for b in range(tm_bits + sp_bits):
            if bits >> b & 1:
                other = flip(other, 2**b)[1]
        every.append((other // spaces, other % spaces))
    one_step = len(every) < ONE_STEP_DEVICES
    friends = near + far

    def lanes(start, size):
        return pl.ds(pl.multiple_of(start, LANES), size)

    orders = []
    for p in range(parts):
        order = [b for b in ORDERS[p % len(ORDERS)] if b < tm_bits]
        orders.append([b for b in range(tm_bits) if b not in order] + order)
    plan = [[flip(me, stride_of(b)) for b in order] for order in orders]

    def part_half(p, k):
        side = plan[p][0][0]
        return p * width + ((1 - side) * half if k == 0 else side * half)

    exps_load = pltpu.make_async_copy(exps_in, exps_ref, exps_sem)
    exps_load.start()
    loads = {}

    def load(p, k):
        at = lanes(part_half(p, k), half)
        loads[p, k] = pltpu.make_async_copy(x_ref.at[:, at], xbuf.at[:, at], x_sem.at[p, k])
        loads[p, k].start()

    load(0, 0)
    barrier = pltpu.get_barrier_semaphore()
    for friend in friends:
        pl.semaphore_signal(barrier, inc=1, device_id=friend, device_id_type=MESH)
    for p in range(1, parts):
        load(p, 0)

    exps_load.wait()
    rate, frequency = column_of(exps_ref[pl.ds(0, 1), :]), column_of(exps_ref[pl.ds(1, 1), :])
    total_rows = local_rows * 2**tm_bits
    steps = lax.broadcasted_iota(jnp.int32, (1, local_rows), 1)
    time = (me * local_rows + steps).astype(jnp.float32) / total_rows
    real, imag = waves(rate, frequency, time)
    plain = jnp.concatenate([real, -imag], 0)
    basis[...] = jnp.concatenate([plain, time * plain], 0).astype(jnp.bfloat16)
    for p in range(parts):
        load(p, 1)

    def project(p, k):
        loads[p, k].wait()
        at = part_half(p, k)
        tile = min(TILE, half)

        def step(i, carry):
            here = lanes(at + i * tile, tile)
            yz_ref[:, here] = jnp.dot(
                basis[...], xbuf[:, here], preferred_element_type=jnp.float32
            )
            return carry

        lax.fori_loop(0, half // tile, step, 0)

    sends = []

    def remote(src, dst, send, recv, friend):
        copy = pltpu.make_async_remote_copy(
            src_ref=src, dst_ref=dst, send_sem=send, recv_sem=recv,
            device_id=friend, device_id_type=MESH,
        )
        copy.start()
        sends.append(copy)
        return copy

    flying = {}
    above = pl.ds(0, double)

    def scatter_start(p, s):
        side, partner = plan[p][s]
        size = width >> (s + 1)
        away = (1 - side) * size
        if s == last:
            src, dst = halves[s - 1].at[p], tail.at[p]
        elif s == 0:
            src, dst = yz_ref.at[above, lanes(p * width + away, size)], halves[s].at[p]
        else:
            src, dst = halves[s - 1].at[p, :, lanes(away, size)], halves[s].at[p]
        flying[p] = remote(src, dst, rs_send.at[p, s], rs_recv.at[p, s], (partner, sp))

    def scatter_add(p, s):
        side, _ = plan[p][s]
        size = width >> (s + 1)
        if s == 0:
            mine = yz_ref[above, lanes(p * width + side * size, size)]
        else:
            mine = halves[s - 1][p, :, lanes(side * size, size)]
        halves[s][p] = halves[s][p] + mine

    offsets = []
    for p in range(parts):
        start = p * width
        for s in range(last):
            start = start + plan[p][s][0] * (width >> (s + 1))
        offsets.append(start)

    def gather_start(p, s):
        where = full.at[:, lanes(offsets[p], width >> (s + 1))]
        flying[p] = remote(
            where, where, ag_send.at[p, s], ag_recv.at[p, s], (plan[p][s][1], sp)
        )

    def gather_sum_start(source, landed, slot, peers, send, recv):
        copies = [
            remote(source, landed.at[slot], send.at[d], recv.at[d], peer)
            for d, peer in enumerate(peers)
        ]
        landed[slot] = source[...]
        return copies

    def gather_sum_end(copies, landed):
        for copy in copies:
            copy.wait_recv()
        total = landed[0]
        for k in range(1, len(copies) + 1):
            total = total + landed[k]
        return total

    for p in range(parts):
        project(p, 0)
        if p == 0:
            pl.semaphore_wait(barrier, len(friends))
        scatter_start(p, 0)

    state = {
        "self": jnp.zeros((double, double), jnp.float32),
        "cross": (jnp.zeros((modes, LANES), jnp.float32),) * 2,
    }
    square = (modes, modes)

    def gram():
        fit_basis[...] = jnp.transpose(plain).astype(jnp.bfloat16)
        base_time = steps.astype(jnp.float32) / total_rows
        base = moments(*waves(rate, frequency, base_time), base_time)
        groups = 2**tm_bits
        wide = max(LANES, groups)
        block = lax.broadcasted_iota(jnp.int32, (1, wide), 1)
        shift_time = (block * local_rows).astype(jnp.float32) / total_rows
        used = block < groups
        shift_time = jnp.where(used, shift_time, 0.0)
        turn_r, turn_i = waves(rate, frequency, shift_time)
        turn = moments(
            jnp.where(used, turn_r, 0.0), jnp.where(used, turn_i, 0.0), shift_time
        )

        def times(m, n):
            return complex_product(*turn[m], *base[n])

        g = times(0, 0)
        c = [a + b for a, b in zip(times(1, 0), times(0, 1))]
        e = [
            a + 2.0 * b + d for a, b, d in zip(times(2, 0), times(1, 1), times(0, 2))
        ]
        state.update(c=c, e=e, inverse=g)

    def finish_inverse():
        inv_r, inv_i = state["inverse"]
        state["solve"] = jnp.concatenate(
            [jnp.concatenate([inv_r, -inv_i], 1), jnp.concatenate([inv_i, inv_r], 1)], 0
        )

    def model():
        c_r, c_i = state["c"]
        t_r, t_i = complex_dot(*state["inverse"], c_r, c_i)
        u_r, u_i = complex_dot(c_r, c_i, t_r, t_i)
        state["m"] = (state["e"][0] - u_r, state["e"][1] - u_i)

    def arrive(p, stage):
        if stage < last:
            flying[p].wait_recv()
            scatter_add(p, stage)
            scatter_start(p, stage + 1)
        elif stage == last:
            flying[p].wait_recv()
            amps = exact_dot(state["solve"], halves[last - 1][p] + tail[p])
            full[:, lanes(offsets[p], width >> last)] = amps
            gather_start(p, last - 1)
            state["self"] = state["self"] + exact_dot(amps, amps, OVER_LANES)
        else:
            s = 2 * last - stage
            flying[p].wait_recv()
            offsets[p] = offsets[p] - plan[p][s][0] * (width >> (s + 1))
            if s > 0:
                gather_start(p, s - 1)

    def sum_start():
        both = state["self"]
        moved = pltpu.roll(jnp.concatenate([both, both], 1), LANES - modes, 1)
        s_r = both[:modes, :modes] + moved[modes:, :modes]
        s_i = moved[:modes, :modes] - both[modes:, :modes]
        pair = 0.5 * jnp.concatenate([s_r, s_i], 1)
        ssum[0] = jnp.concatenate([pair[: modes // 2], pair[modes // 2 :]], 1)
        state["copies"] = gather_sum_start(ssum.at[0], snear, near_slot, near, sn_send, sn_recv)

    def sum_near():
        ssum[1] = gather_sum_end(state["copies"], snear)
        state["copies"] = gather_sum_start(ssum.at[1], sfar, far_slot, far, sf_send, sf_recv)

    def sum_far():
        packed = gather_sum_end(state["copies"], sfar)

        def piece(n):
            moved = packed if n == 0 else pltpu.roll(packed, LANES - n * modes, 1)
            return moved[:, :modes]

        s_r = jnp.concatenate([piece(0), piece(2)], 0)
        s_i = jnp.concatenate([piece(1), piece(3)], 0)
        diagonal = lax.broadcasted_iota(jnp.int32, square, 0) == lax.broadcasted_iota(
            jnp.int32, square, 1
        )
        h_r, h_i = complex_product(s_r, s_i, *state["m"])
        c_r, c_i = state["c"]
        state["hessian"] = (h_r + jnp.where(diagonal, damping, 0.0), h_i)
        state["w"] = (
            jnp.sum(c_r * s_r - c_i * s_i, 1, keepdims=True),
            jnp.sum(c_r * s_i + c_i * s_r, 1, keepdims=True),
        )

    def fit_start(p, k):
        return part_half(p, 1 - k)

    def cross(p, k):
        start = fit_start(p, k)
        run = min(4, half // LANES)

        def step(i, carry):
            v_r, v_i = carry
            for j in range(run):
                at = lanes(start + (i * run + j) * LANES, LANES)
                a_r, a_i = full[pl.ds(0, modes), at], full[pl.ds(modes, modes), at]
                z_r = yz_ref[pl.ds(double, modes), at]
                z_i = yz_ref[pl.ds(double + modes, modes), at]
                v_r = v_r + (a_r * z_r + a_i * z_i)
                v_i = v_i + (a_r * z_i - a_i * z_r)
            return v_r, v_i

        state["cross"] = lax.fori_loop(0, half // (run * LANES), step, state["cross"])

    fit_jobs = max(half // FIT_TILE, 1)
    fit_tile = half // fit_jobs

    def fit(p, k, i):
        at = lanes(fit_start(p, k) + i * fit_tile, fit_tile)
        fitted = jnp.dot(
            fit_basis[...], full[:, at].astype(jnp.bfloat16), preferred_element_type=jnp.float32
        )
        res_ref[:, at] = (xbuf[:, at].astype(jnp.float32) - fitted).astype(res_ref.dtype)

    def cross_sum():
        ones = jnp.ones((8, LANES), jnp.float32)
        vsum[0] = jnp.zeros(vsum.shape[1:], jnp.float32)
        vsum[0, :, pl.ds(0, double)] = exact_dot(
            ones, jnp.concatenate(state["cross"], 0), OVER_LANES
        )
        slot, peers = (every_slot, every) if one_step else (near_slot, near)
        state["v"] = gather_sum_start(vsum.at[0], vnear, slot, peers, n_send, n_recv)

    def cross_near():
        if not one_step:
            vsum[1] = gather_sum_end(state["v"], vnear)
            state["v"] = gather_sum_start(vsum.at[1], vfar, far_slot, far, f_send, f_recv)

    invert_jobs = modes // INVERT_STEPS
    script = timeline(orders, tm_bits, width, double, invert_jobs, fit_jobs)
    at_sum = script.index(("cross_sum",))
    trailing = [i for i, job in enumerate(script) if i > at_sum and job[0] in ("fit", "hessian")]
    middle = trailing[len(trailing) // 2] if trailing else None
    passed = False
    for i, (name, *where) in enumerate(script):
        if i == middle:
            cross_near()
            passed = True
        if name == "arrive":
            arrive(*where)
        elif name == "rest":
            project(where[0], 1)
        elif name == "gram":
            gram()
        elif name == "invert":
            state["inverse"] = invert_steps(
                *state["inverse"], where[0] * INVERT_STEPS, INVERT_STEPS
            )
            if where[0] == invert_jobs - 1:
                finish_inverse()
        elif name == "hessian":
            state["hessian"] = invert_steps(
                *state["hessian"], where[0] * INVERT_STEPS, INVERT_STEPS
            )
        elif name == "model":
            model()
        elif name == "sum":
            sum_start()
        elif name == "sum_near":
            sum_near()
        elif name == "sum_far":
            sum_far()
        elif name == "cross":
            cross(*where)
        elif name == "fit":
            fit(*where)
        elif name == "cross_sum":
            cross_sum()
    if not passed:
        cross_near()
    for copy in sends:
        copy.wait_send()
    v_all = gather_sum_end(state["v"], vnear if one_step else vfar)[:1]

    wide = (modes, LANES)
    spread = lax.broadcasted_iota(jnp.int32, wide, 1) - lax.broadcasted_iota(jnp.int32, wide, 0)

    def as_column(shift):
        return jnp.sum(jnp.where(spread == shift, v_all, 0.0), 1, keepdims=True)

    grad_r = state["w"][0] - as_column(0)
    grad_i = state["w"][1] - as_column(modes)
    hinv_r, hinv_i = state["hessian"]
    new_ref[pl.ds(0, 1), :] = exps_ref[pl.ds(0, 1), :] - jnp.sum(
        hinv_r * grad_r + hinv_i * grad_i, 0, keepdims=True
    )
    new_ref[pl.ds(1, 1), :] = exps_ref[pl.ds(1, 1), :] - jnp.sum(
        hinv_r * grad_i - hinv_i * grad_r, 0, keepdims=True
    )


def step(snapshots, exponents, groups, spaces):
    modes = exponents.shape[1]
    double = 2 * modes
    local_rows, columns = snapshots.shape
    tm_bits, sp_bits = groups.bit_length() - 1, spaces.bit_length() - 1
    assert groups == 2**tm_bits and spaces == 2**sp_bits and tm_bits >= 2
    assert 4 * modes == LANES
    parts = min(len(ORDERS), columns // (groups // 2 * LANES))
    width = columns // parts
    low = 2 ** (tm_bits // 2)
    near, far = low * spaces, groups // low
    every = groups * spaces
    v_near = every if every <= ONE_STEP_DEVICES else near

    def buffer(*shape):
        return pltpu.VMEM(shape, jnp.float32)

    def dma(*shape):
        return pltpu.SemaphoreType.DMA(shape)

    vmem = pl.BlockSpec(memory_space=pltpu.VMEM)
    return pl.pallas_call(
        functools.partial(step_kernel, modes, tm_bits, sp_bits, parts),
        out_shape=(
            jax.ShapeDtypeStruct((double, columns), jnp.float32),
            jax.ShapeDtypeStruct(snapshots.shape, snapshots.dtype),
            jax.ShapeDtypeStruct(exponents.shape, jnp.float32),
        ),
        in_specs=[pl.BlockSpec(memory_space=pltpu.HBM)] * 2,
        out_specs=(vmem, vmem, vmem),
        scratch_shapes=[
            buffer(*exponents.shape),
            pltpu.VMEM((local_rows, columns), snapshots.dtype),
            buffer(2 * double, columns),
            pltpu.VMEM((2 * double, local_rows), jnp.bfloat16),
            pltpu.VMEM((local_rows, double), jnp.bfloat16),
            [buffer(parts, double, width >> (s + 1)) for s in range(tm_bits - 1)],
            buffer(parts, double, width >> (tm_bits - 1)),
            buffer(2, modes // 2, LANES),
            buffer(near, modes // 2, LANES),
            buffer(far, modes // 2, LANES),
            buffer(2, 8, LANES),
            buffer(v_near, 8, LANES),
            buffer(far, 8, LANES),
            dma(parts, tm_bits), dma(parts, tm_bits),
            dma(parts, tm_bits), dma(parts, tm_bits),
            dma(near - 1), dma(near - 1),
            dma(far - 1), dma(far - 1),
            dma(v_near - 1), dma(v_near - 1),
            dma(far - 1), dma(far - 1),
            dma(parts, 2),
            pltpu.SemaphoreType.DMA,
        ],
        compiler_params=pltpu.CompilerParams(
            collective_id=0, has_side_effects=True, vmem_limit_bytes=40 * 2**20
        ),
    )(snapshots, exponents)


def write_kernel(pieces, *refs):
    sources, targets, sem = refs[:3], refs[3:6], refs[6]
    copies = []
    for i, (source, target) in enumerate(zip(sources, targets)):
        rows = source.shape[0] // pieces[i]
        for j in range(pieces[i]):
            part = pl.ds(j * rows, rows)
            copies.append((source.at[part], target.at[part]))
    copies = [
        pltpu.make_async_copy(source, target, sem.at[i])
        for i, (source, target) in enumerate(copies)
    ]
    for copy in copies:
        copy.start()
    for copy in copies:
        copy.wait()


def write(residual, amp_rows, new_exponents):
    pieces = (8, 2, 1)
    arrays = (residual, amp_rows, new_exponents)
    return pl.pallas_call(
        functools.partial(write_kernel, pieces),
        out_shape=tuple(jax.ShapeDtypeStruct(a.shape, a.dtype) for a in arrays),
        in_specs=[pl.BlockSpec(memory_space=pltpu.VMEM)] * 3,
        out_specs=[pl.BlockSpec(memory_space=pltpu.HBM)] * 3,
        scratch_shapes=[pltpu.SemaphoreType.DMA((sum(pieces),))],
        compiler_params=pltpu.CompilerParams(vmem_limit_bytes=24 * 2**20),
    )(*arrays)


def shards(snapshots, exponents):
    columns = snapshots.shape[1]
    modes = exponents.shape[1]
    groups, spaces = lax.axis_size("tm"), lax.axis_size("space")
    amp_rows, residual, new_exponents = step(snapshots, exponents, groups, spaces)
    residual, amp_rows, new_exponents = write(residual, amp_rows, new_exponents)
    return (new_exponents, amp_rows.reshape(2, modes, columns), residual)


def solution(mesh):
    return jax.shard_map(
        shards,
        mesh=mesh,
        in_specs=(P("tm", "space"), P()),
        out_specs=(P(), P(None, None, "space"), P("tm", "space")),
        check_vma=False,
    )
```

```python
import functools
import heapq

import jax
import jax.numpy as jnp
from jax import lax
from jax.experimental import pallas as pl
from jax.experimental.pallas import tpu as pltpu
from jax.sharding import PartitionSpec as P

damping = 0.01
MESH = pl.DeviceIdType.MESH
LANES = 128
TILE = 512
FIT_TILE = 512
INVERT_STEPS = 2
ORDERS = (
    (3, 0, 2, 1), (0, 2, 1, 3), (0, 1, 2, 3), (1, 0, 3, 2), (0, 1, 3, 2), (2, 0, 1, 3), (2, 0, 1, 3), (0, 1, 2, 3),
)
ONE_STEP_DEVICES = 32
OVER_LANES = ((1,), (1,))

LINK_BYTES_PER_US = 94e3
HOP_US = 2.45
FAR_US = 0.42
STEP_US = 0.4
PROJECT_US = 0.25
AMPLITUDE_US = 0.45
GRAM_US = 1.0
INVERT_US = 0.18
MODEL_US = 0.6
CROSS_US = 0.05
FIT_US = 0.4
SLACK_US = 0.1
START_US = 2.3


def exact_dot(left, right, dims=((1,), (0,))):
    return lax.dot_general(
        left,
        right,
        (dims, ((), ())),
        precision=lax.Precision.HIGHEST,
        preferred_element_type=jnp.float32,
    )


def complex_dot(ar, ai, br, bi):
    return exact_dot(ar, br) - exact_dot(ai, bi), exact_dot(ar, bi) + exact_dot(ai, br)


def complex_product(ar, ai, br, bi):
    return ar * br - ai * bi, ar * bi + ai * br


def invert_steps(real, imag, first, count):
    rows = lax.broadcasted_iota(jnp.int32, real.shape, 0)
    cols = lax.broadcasted_iota(jnp.int32, real.shape, 1)
    for k in range(first, first + count):
        on_row, on_col = rows == k, cols == k
        scale = 1.0 / real[k : k + 1, k : k + 1]
        row_r = jnp.where(on_col[:1], 1.0, real[k : k + 1, :]) * scale
        row_i = jnp.where(on_col[:1], 0.0, imag[k : k + 1, :]) * scale
        col_r, col_i = real[:, k : k + 1], imag[:, k : k + 1]
        real = jnp.where(
            on_row, row_r, jnp.where(on_col, 0.0, real) - (col_r * row_r - col_i * row_i)
        )
        imag = jnp.where(
            on_row, row_i, jnp.where(on_col, 0.0, imag) - (col_r * row_i + col_i * row_r)
        )
    return real, imag


def column_of(row):
    n = row.shape[1]
    here = lax.broadcasted_iota(jnp.int32, (n, n), 0) == lax.broadcasted_iota(
        jnp.int32, (n, n), 1
    )
    return jnp.sum(jnp.where(here, row, 0.0), 1, keepdims=True)


def waves(rate, frequency, time):
    magnitude = jnp.exp(time * rate)
    angle = time * frequency
    return magnitude * jnp.cos(angle), magnitude * jnp.sin(angle)


def moments(real, imag, time):
    modes = real.shape[0]
    both = jnp.concatenate(
        [jnp.concatenate([real, imag], 1), jnp.concatenate([-imag, real], 1)], 0
    )
    first, twice = both[:modes], jnp.concatenate([time, time], 1)
    powers = [first, twice * first, twice * (twice * first)]
    powers += [jnp.zeros_like(first)] * (LANES // modes - len(powers))
    sums = exact_dot(both, jnp.concatenate(powers, 0), OVER_LANES)
    blocks = []
    for n in range(3):
        moved = sums if n == 0 else pltpu.roll(sums, LANES - n * modes, 1)
        blocks.append((moved[:modes, :modes], moved[modes:, :modes]))
    return blocks


def timeline(orders, bits, width, rows, invert_jobs, fit_jobs):
    parts, last = len(orders), 2 * bits - 2
    free = {}
    events, script, count = [], [], [0]
    done = set()
    now = START_US

    def post(at, what):
        heapq.heappush(events, (at, count[0], what))
        count[0] += 1

    def send(p, stage):
        s = min(stage, last - stage)
        bit = orders[p][s]
        size = (width >> min(s + 1, bits - 1)) * rows * 4 / LINK_BYTES_PER_US
        delay = HOP_US
        if bit < 2:
            keys = {"xy": size}
        elif bit == 2:
            keys = {"near": 2 * size}
        else:
            keys, delay = {"near": 2 * size, "far": 4 * size}, HOP_US + FAR_US
        start = max([now] + [free.get(k, 0.0) for k in keys])
        for k, v in keys.items():
            free[k] = start + v
        post(start + max(keys.values()) + delay, ("arrive", p, stage))

    for p in range(parts):
        now += PROJECT_US
        send(p, 0)
    jobs = [("rest", p) for p in range(parts)] + [("gram",)]
    jobs += [("invert", i) for i in range(invert_jobs)] + [("model",)]
    cost = {
        "rest": PROJECT_US, "gram": GRAM_US, "invert": INVERT_US, "model": MODEL_US,
        "hessian": INVERT_US, "cross": CROSS_US, "fit": FIT_US,
    }
    rank = {
        "rest": 0, "gram": 1, "invert": 2, "cross": 3, "hessian": 4, "model": 5, "fit": 6,
    }

    def run(job):
        nonlocal now
        jobs.remove(job)
        done.add(job)
        script.append(job)
        now += cost[job[0]]

    amplitudes = crossed = 0
    while events or jobs:
        if events and (events[0][0] <= now or not jobs):
            at, _, what = heapq.heappop(events)
            now = max(now, at)
            if what[0] == "arrive":
                _, p, stage = what
                if stage == 0 and ("rest", p) not in done:
                    run(("rest", p))
                if stage == bits - 1:
                    for job in [j for j in jobs if j[0] in ("gram", "invert")]:
                        run(job)
                    now += AMPLITUDE_US
                    amplitudes += 1
                script.append(what)
                now += STEP_US
                if stage < last:
                    send(p, stage + 1)
                if stage >= last - 1:
                    k = stage - (last - 1)
                    jobs += [("cross", p, k)] + [("fit", p, k, i) for i in range(fit_jobs)]
                if amplitudes == parts and ("sum",) not in done:
                    done.add(("sum",))
                    script.append(("sum",))
                    now += AMPLITUDE_US
                    post(max([now, *free.values()]) + HOP_US + 1.0, ("sum_near",))
            elif what[0] == "sum_near":
                script.append(what)
                now += STEP_US
                post(max([now, *free.values()]) + HOP_US + 1.5, ("sum_far",))
            else:
                script.append(what)
                if ("model",) in jobs:
                    jobs.remove(("model",))
                    script.insert(len(script) - 1, ("model",))
                jobs += [("hessian", i) for i in range(invert_jobs)]
            continue
        job = min(jobs, key=lambda j: rank[j[0]])
        if events and rank[job[0]] > 0 and events[0][0] < now + cost[job[0]] - SLACK_US:
            now = max(now, events[0][0])
            continue
        run(job)
        if job[0] == "cross":
            crossed += 1
            if crossed == 2 * parts:
                script.append(("cross_sum",))
    at, known = script.index(("cross_sum",)), script.index(("sum_far",))
    if known > at:
        script.insert(known, script.pop(at))
    return script


def step_kernel(
    modes, tm_bits, sp_bits, parts,
    x_ref, exps_in,
    full, res_ref, new_ref,
    exps_ref, xbuf, yz_ref, basis, fit_basis, halves, tail, ssum, snear, sfar, vsum, vnear, vfar,
    rs_send, rs_recv, ag_send, ag_recv,
    sn_send, sn_recv, sf_send, sf_recv, n_send, n_recv, f_send, f_recv, x_sem, exps_sem,
):
    double = 2 * modes
    local_rows, columns = xbuf.shape
    width = columns // parts
    half = width // 2
    last = tm_bits - 1
    me, sp = lax.axis_index("tm"), lax.axis_index("space")
    swap = sp % 2

    def stride_of(bit):
        if tm_bits > 2 and bit == 0:
            return 1 + swap
        if tm_bits > 2 and bit == 1:
            return 2 - swap
        return 2**bit

    def flip(index, stride):
        side = (index // stride) % 2
        return side, index + (1 - 2 * side) * stride

    spaces, low = 2**sp_bits, 2 ** (tm_bits // 2)
    n_near, n_far = low * spaces, 2**tm_bits // low
    near_slot, far_slot = (me % low) * spaces + sp, me // low
    near, far = [], []
    for d in range(1, n_near):
        other = (near_slot + d) % n_near
        near.append((far_slot * low + other // spaces, other % spaces))
    for d in range(1, n_far):
        far.append(((far_slot + d) % n_far * low + me % low, sp))
    n_all = 2**tm_bits * spaces
    every, every_slot = [], me * spaces + sp
    for bits in range(n_all - 1, 0, -1):
        other = every_slot
        for b in range(tm_bits + sp_bits):
            if bits >> b & 1:
                other = flip(other, 2**b)[1]
        every.append((other // spaces, other % spaces))
    one_step = len(every) < ONE_STEP_DEVICES
    friends = near + far

    def lanes(start, size):
        return pl.ds(pl.multiple_of(start, LANES), size)

    orders = []
    for p in range(parts):
        order = [b for b in ORDERS[p % len(ORDERS)] if b < tm_bits]
        orders.append([b for b in range(tm_bits) if b not in order] + order)
    plan = [[flip(me, stride_of(b)) for b in order] for order in orders]

    def part_half(p, k):
        side = plan[p][0][0]
        return p * width + ((1 - side) * half if k == 0 else side * half)

    exps_load = pltpu.make_async_copy(exps_in, exps_ref, exps_sem)
    exps_load.start()
    loads = {}

    def load(p, k):
        at = lanes(part_half(p, k), half)
        loads[p, k] = pltpu.make_async_copy(x_ref.at[:, at], xbuf.at[:, at], x_sem.at[p, k])
        loads[p, k].start()

    load(0, 0)
    barrier = pltpu.get_barrier_semaphore()
    for friend in friends:
        pl.semaphore_signal(barrier, inc=1, device_id=friend, device_id_type=MESH)
    for p in range(1, parts):
        load(p, 0)

    exps_load.wait()
    rate, frequency = column_of(exps_ref[pl.ds(0, 1), :]), column_of(exps_ref[pl.ds(1, 1), :])
    total_rows = local_rows * 2**tm_bits
    steps = lax.broadcasted_iota(jnp.int32, (1, local_rows), 1)
    time = (me * local_rows + steps).astype(jnp.float32) / total_rows
    real, imag = waves(rate, frequency, time)
    plain = jnp.concatenate([real, -imag], 0)
    basis[...] = jnp.concatenate([plain, time * plain], 0).astype(jnp.bfloat16)
    for p in range(parts):
        load(p, 1)

    def project(p, k):
        loads[p, k].wait()
        at = part_half(p, k)
        tile = min(TILE, half)

        def step(i, carry):
            here = lanes(at + i * tile, tile)
            yz_ref[:, here] = jnp.dot(
                basis[...], xbuf[:, here], preferred_element_type=jnp.float32
            )
            return carry

        lax.fori_loop(0, half // tile, step, 0)

    sends = []

    def remote(src, dst, send, recv, friend):
        copy = pltpu.make_async_remote_copy(
            src_ref=src, dst_ref=dst, send_sem=send, recv_sem=recv,
            device_id=friend, device_id_type=MESH,
        )
        copy.start()
        sends.append(copy)
        return copy

    flying = {}
    above = pl.ds(0, double)

    def scatter_start(p, s):
        side, partner = plan[p][s]
        size = width >> (s + 1)
        away = (1 - side) * size
        if s == last:
            src, dst = halves[s - 1].at[p], tail.at[p]
        elif s == 0:
            src, dst = yz_ref.at[above, lanes(p * width + away, size)], halves[s].at[p]
        else:
            src, dst = halves[s - 1].at[p, :, lanes(away, size)], halves[s].at[p]
        flying[p] = remote(src, dst, rs_send.at[p, s], rs_recv.at[p, s], (partner, sp))

    def scatter_add(p, s):
        side, _ = plan[p][s]
        size = width >> (s + 1)
        if s == 0:
            mine = yz_ref[above, lanes(p * width + side * size, size)]
        else:
            mine = halves[s - 1][p, :, lanes(side * size, size)]
        halves[s][p] = halves[s][p] + mine

    offsets = []
    for p in range(parts):
        start = p * width
        for s in range(last):
            start = start + plan[p][s][0] * (width >> (s + 1))
        offsets.append(start)

    def gather_start(p, s):
        where = full.at[:, lanes(offsets[p], width >> (s + 1))]
        flying[p] = remote(
            where, where, ag_send.at[p, s], ag_recv.at[p, s], (plan[p][s][1], sp)
        )

    def gather_sum_start(source, landed, slot, peers, send, recv):
        copies = [
            remote(source, landed.at[slot], send.at[d], recv.at[d], peer)
            for d, peer in enumerate(peers)
        ]
        landed[slot] = source[...]
        return copies

    def gather_sum_end(copies, landed):
        for copy in copies:
            copy.wait_recv()
        total = landed[0]
        for k in range(1, len(copies) + 1):
            total = total + landed[k]
        return total

    for p in range(parts):
        project(p, 0)
        if p == 0:
            pl.semaphore_wait(barrier, len(friends))
        scatter_start(p, 0)

    state = {
        "self": jnp.zeros((double, double), jnp.float32),
        "cross": (jnp.zeros((modes, LANES), jnp.float32),) * 2,
    }
    square = (modes, modes)

    def gram():
        fit_basis[...] = jnp.transpose(plain).astype(jnp.bfloat16)
        base_time = steps.astype(jnp.float32) / total_rows
        base = moments(*waves(rate, frequency, base_time), base_time)
        groups = 2**tm_bits
        wide = max(LANES, groups)
        block = lax.broadcasted_iota(jnp.int32, (1, wide), 1)
        shift_time = (block * local_rows).astype(jnp.float32) / total_rows
        used = block < groups
        shift_time = jnp.where(used, shift_time, 0.0)
        turn_r, turn_i = waves(rate, frequency, shift_time)
        turn = moments(
            jnp.where(used, turn_r, 0.0), jnp.where(used, turn_i, 0.0), shift_time
        )

        def times(m, n):
            return complex_product(*turn[m], *base[n])

        g = times(0, 0)
        c = [a + b for a, b in zip(times(1, 0), times(0, 1))]
        e = [
            a + 2.0 * b + d for a, b, d in zip(times(2, 0), times(1, 1), times(0, 2))
        ]
        state.update(c=c, e=e, inverse=g)

    def finish_inverse():
        inv_r, inv_i = state["inverse"]
        state["solve"] = jnp.concatenate(
            [jnp.concatenate([inv_r, -inv_i], 1), jnp.concatenate([inv_i, inv_r], 1)], 0
        )

    def model():
        c_r, c_i = state["c"]
        t_r, t_i = complex_dot(*state["inverse"], c_r, c_i)
        u_r, u_i = complex_dot(c_r, c_i, t_r, t_i)
        state["m"] = (state["e"][0] - u_r, state["e"][1] - u_i)

    def arrive(p, stage):
        if stage < last:
            flying[p].wait_recv()
            scatter_add(p, stage)
            scatter_start(p, stage + 1)
        elif stage == last:
            flying[p].wait_recv()
            amps = exact_dot(state["solve"], halves[last - 1][p] + tail[p])
            full[:, lanes(offsets[p], width >> last)] = amps
            gather_start(p, last - 1)
            state["self"] = state["self"] + exact_dot(amps, amps, OVER_LANES)
        else:
            s = 2 * last - stage
            flying[p].wait_recv()
            offsets[p] = offsets[p] - plan[p][s][0] * (width >> (s + 1))
            if s > 0:
                gather_start(p, s - 1)

    def sum_start():
        both = state["self"]
        moved = pltpu.roll(jnp.concatenate([both, both], 1), LANES - modes, 1)
        s_r = both[:modes, :modes] + moved[modes:, :modes]
        s_i = moved[:modes, :modes] - both[modes:, :modes]
        pair = 0.5 * jnp.concatenate([s_r, s_i], 1)
        ssum[0] = jnp.concatenate([pair[: modes // 2], pair[modes // 2 :]], 1)
        state["copies"] = gather_sum_start(ssum.at[0], snear, near_slot, near, sn_send, sn_recv)

    def sum_near():
        ssum[1] = gather_sum_end(state["copies"], snear)
        state["copies"] = gather_sum_start(ssum.at[1], sfar, far_slot, far, sf_send, sf_recv)

    def sum_far():
        packed = gather_sum_end(state["copies"], sfar)

        def piece(n):
            moved = packed if n == 0 else pltpu.roll(packed, LANES - n * modes, 1)
            return moved[:, :modes]

        s_r = jnp.concatenate([piece(0), piece(2)], 0)
        s_i = jnp.concatenate([piece(1), piece(3)], 0)
        diagonal = lax.broadcasted_iota(jnp.int32, square, 0) == lax.broadcasted_iota(
            jnp.int32, square, 1
        )
        h_r, h_i = complex_product(s_r, s_i, *state["m"])
        c_r, c_i = state["c"]
        state["hessian"] = (h_r + jnp.where(diagonal, damping, 0.0), h_i)
        state["w"] = (
            jnp.sum(c_r * s_r - c_i * s_i, 1, keepdims=True),
            jnp.sum(c_r * s_i + c_i * s_r, 1, keepdims=True),
        )

    def fit_start(p, k):
        return part_half(p, 1 - k)

    def cross(p, k):
        start = fit_start(p, k)
        run = min(4, half // LANES)

        def step(i, carry):
            v_r, v_i = carry
            for j in range(run):
                at = lanes(start + (i * run + j) * LANES, LANES)
                a_r, a_i = full[pl.ds(0, modes), at], full[pl.ds(modes, modes), at]
                z_r = yz_ref[pl.ds(double, modes), at]
                z_i = yz_ref[pl.ds(double + modes, modes), at]
                v_r = v_r + (a_r * z_r + a_i * z_i)
                v_i = v_i + (a_r * z_i - a_i * z_r)
            return v_r, v_i

        state["cross"] = lax.fori_loop(0, half // (run * LANES), step, state["cross"])

    fit_jobs = max(half // FIT_TILE, 1)
    fit_tile = half // fit_jobs

    def fit(p, k, i):
        at = lanes(fit_start(p, k) + i * fit_tile, fit_tile)
        fitted = jnp.dot(
            fit_basis[...], full[:, at].astype(jnp.bfloat16), preferred_element_type=jnp.float32
        )
        res_ref[:, at] = (xbuf[:, at].astype(jnp.float32) - fitted).astype(res_ref.dtype)

    def cross_sum():
        ones = jnp.ones((8, LANES), jnp.float32)
        vsum[0] = jnp.zeros(vsum.shape[1:], jnp.float32)
        vsum[0, :, pl.ds(0, double)] = exact_dot(
            ones, jnp.concatenate(state["cross"], 0), OVER_LANES
        )
        slot, peers = (every_slot, every) if one_step else (near_slot, near)
        state["v"] = gather_sum_start(vsum.at[0], vnear, slot, peers, n_send, n_recv)

    def cross_near():
        if not one_step:
            vsum[1] = gather_sum_end(state["v"], vnear)
            state["v"] = gather_sum_start(vsum.at[1], vfar, far_slot, far, f_send, f_recv)

    invert_jobs = modes // INVERT_STEPS
    script = timeline(orders, tm_bits, width, double, invert_jobs, fit_jobs)
    at_sum = script.index(("cross_sum",))
    trailing = [i for i, job in enumerate(script) if i > at_sum and job[0] in ("fit", "hessian")]
    middle = trailing[len(trailing) // 2] if trailing else None
    passed = False
    for i, (name, *where) in enumerate(script):
        if i == middle:
            cross_near()
            passed = True
        if name == "arrive":
            arrive(*where)
        elif name == "rest":
            project(where[0], 1)
        elif name == "gram":
            gram()
        elif name == "invert":
            state["inverse"] = invert_steps(
                *state["inverse"], where[0] * INVERT_STEPS, INVERT_STEPS
            )
            if where[0] == invert_jobs - 1:
                finish_inverse()
        elif name == "hessian":
            state["hessian"] = invert_steps(
                *state["hessian"], where[0] * INVERT_STEPS, INVERT_STEPS
            )
        elif name == "model":
            model()
        elif name == "sum":
            sum_start()
        elif name == "sum_near":
            sum_near()
        elif name == "sum_far":
            sum_far()
        elif name == "cross":
            cross(*where)
        elif name == "fit":
            fit(*where)
        elif name == "cross_sum":
            cross_sum()
    if not passed:
        cross_near()
    for copy in sends:
        copy.wait_send()
    v_all = gather_sum_end(state["v"], vnear if one_step else vfar)[:1]

    wide = (modes, LANES)
    spread = lax.broadcasted_iota(jnp.int32, wide, 1) - lax.broadcasted_iota(jnp.int32, wide, 0)

    def as_column(shift):
        return jnp.sum(jnp.where(spread == shift, v_all, 0.0), 1, keepdims=True)

    grad_r = state["w"][0] - as_column(0)
    grad_i = state["w"][1] - as_column(modes)
    hinv_r, hinv_i = state["hessian"]
    new_ref[pl.ds(0, 1), :] = exps_ref[pl.ds(0, 1), :] - jnp.sum(
        hinv_r * grad_r + hinv_i * grad_i, 0, keepdims=True
    )
    new_ref[pl.ds(1, 1), :] = exps_ref[pl.ds(1, 1), :] - jnp.sum(
        hinv_r * grad_i - hinv_i * grad_r, 0, keepdims=True
    )


def step(snapshots, exponents, groups, spaces):
    modes = exponents.shape[1]
    double = 2 * modes
    local_rows, columns = snapshots.shape
    tm_bits, sp_bits = groups.bit_length() - 1, spaces.bit_length() - 1
    assert groups == 2**tm_bits and spaces == 2**sp_bits and tm_bits >= 2
    assert 4 * modes == LANES
    parts = min(len(ORDERS), columns // (groups // 2 * LANES))
    width = columns // parts
    low = 2 ** (tm_bits // 2)
    near, far = low * spaces, groups // low
    every = groups * spaces
    v_near = every if every <= ONE_STEP_DEVICES else near

    def buffer(*shape):
        return pltpu.VMEM(shape, jnp.float32)

    def dma(*shape):
        return pltpu.SemaphoreType.DMA(shape)

    vmem = pl.BlockSpec(memory_space=pltpu.VMEM)
    return pl.pallas_call(
        functools.partial(step_kernel, modes, tm_bits, sp_bits, parts),
        out_shape=(
            jax.ShapeDtypeStruct((double, columns), jnp.float32),
            jax.ShapeDtypeStruct(snapshots.shape, snapshots.dtype),
            jax.ShapeDtypeStruct(exponents.shape, jnp.float32),
        ),
        in_specs=[pl.BlockSpec(memory_space=pltpu.HBM)] * 2,
        out_specs=(vmem, vmem, vmem),
        scratch_shapes=[
            buffer(*exponents.shape),
            pltpu.VMEM((local_rows, columns), snapshots.dtype),
            buffer(2 * double, columns),
            pltpu.VMEM((2 * double, local_rows), jnp.bfloat16),
            pltpu.VMEM((local_rows, double), jnp.bfloat16),
            [buffer(parts, double, width >> (s + 1)) for s in range(tm_bits - 1)],
            buffer(parts, double, width >> (tm_bits - 1)),
            buffer(2, modes // 2, LANES),
            buffer(near, modes // 2, LANES),
            buffer(far, modes // 2, LANES),
            buffer(2, 8, LANES),
            buffer(v_near, 8, LANES),
            buffer(far, 8, LANES),
            dma(parts, tm_bits), dma(parts, tm_bits),
            dma(parts, tm_bits), dma(parts, tm_bits),
            dma(near - 1), dma(near - 1),
            dma(far - 1), dma(far - 1),
            dma(v_near - 1), dma(v_near - 1),
            dma(far - 1), dma(far - 1),
            dma(parts, 2),
            pltpu.SemaphoreType.DMA,
        ],
        compiler_params=pltpu.CompilerParams(
            collective_id=0, has_side_effects=True, vmem_limit_bytes=40 * 2**20
        ),
    )(snapshots, exponents)


def write_kernel(pieces, *refs):
    sources, targets, sem = refs[:3], refs[3:6], refs[6]
    copies = []
    for i, (source, target) in enumerate(zip(sources, targets)):
        rows = source.shape[0] // pieces[i]
        for j in range(pieces[i]):
            part = pl.ds(j * rows, rows)
            copies.append((source.at[part], target.at[part]))
    copies = [
        pltpu.make_async_copy(source, target, sem.at[i])
        for i, (source, target) in enumerate(copies)
    ]
    for copy in copies:
        copy.start()
    for copy in copies:
        copy.wait()


def write(residual, amp_rows, new_exponents):
    pieces = (8, 2, 1)
    arrays = (residual, amp_rows, new_exponents)
    return pl.pallas_call(
        functools.partial(write_kernel, pieces),
        out_shape=tuple(jax.ShapeDtypeStruct(a.shape, a.dtype) for a in arrays),
        in_specs=[pl.BlockSpec(memory_space=pltpu.VMEM)] * 3,
        out_specs=[pl.BlockSpec(memory_space=pltpu.HBM)] * 3,
        scratch_shapes=[pltpu.SemaphoreType.DMA((sum(pieces),))],
        compiler_params=pltpu.CompilerParams(vmem_limit_bytes=24 * 2**20),
    )(*arrays)


def shards(snapshots, exponents):
    columns = snapshots.shape[1]
    modes = exponents.shape[1]
    groups, spaces = lax.axis_size("tm"), lax.axis_size("space")
    amp_rows, residual, new_exponents = step(snapshots, exponents, groups, spaces)
    residual, amp_rows, new_exponents = write(residual, amp_rows, new_exponents)
    return (new_exponents, amp_rows.reshape(2, modes, columns), residual)


def solution(mesh):
    return jax.shard_map(
        shards,
        mesh=mesh,
        in_specs=(P("tm", "space"), P()),
        out_specs=(P(), P(None, None, "space"), P("tm", "space")),
        check_vma=False,
    )
```
